32 devices in a mesh: grp: 2 (over core), ctx: 16 (over z, y, x).
Axes of the slice: x: 2, y: 2, z: 4, core: 2. Of those that a mesh axis runs over, the one named last changes fastest.
Arguments:
- gla_query: bfloat16 [4096, 4096], P(('grp', 'ctx')), parts along dimension 0, may hold values from -6 to 6
- gla_key: bfloat16 [4096, 4096], P(('grp', 'ctx')), parts along dimension 0, may hold values from -6 to 6
- gla_value: bfloat16 [4096, 4096], P(('grp', 'ctx')), parts along dimension 0, may hold values from -6 to 6
- log_gates: float32 [4096, 32], P(('grp', 'ctx')), parts along dimension 0, may hold values from -1.2 to 0
- norm_gain: float32 [4096], replicated, may hold values from 0.5 to 1.5
- attn_query: bfloat16 [4096, 4096], P(('grp', 'ctx')), parts along dimension 0, may hold values from -6 to 6
- attn_key: bfloat16 [4096, 4096], P(('grp', 'ctx')), parts along dimension 0, may hold values from -4 to 4
- doc_blocks: int32 [16], P('grp'), parts along dimension 0, may hold values from 1 to 8, 16 in all
Outputs:
- gla_mixed: bfloat16 [4096, 4096], P(('grp', 'ctx')), parts along dimension 0
- attended: bfloat16 [4096, 4096], P(('grp', 'ctx')), parts along dimension 0
The draws below stay inside these ranges and needn't reach their ends.
There are 2 independent parts, one for each index of `grp`. The reference program is written for one: setup_inputs(seed, part) draws one part's arguments, and reference() takes and returns one part's arrays. A program takes and returns all parts, laid end to end along the dimension named above; an argument that names none is the same for every part. Nothing has to cross between parts.
Inputs may be any that keep to these rules, and one draw needn't show every extreme that they name: `doc_blocks`: the documents of a group in order, together covering all 2048 tokens; the longest has exactly 8 blocks.
All inputs are finite; a program needn't handle non-finite values.
Results may differ from the reference program's by a relative error of at most 0.0057.
Values may be sent and summed in bfloat16 or wider, within the bound.
No kernel may reach another device: no remote copies, remote signals or barrier semaphores. Data moves between devices by JAX's collectives and lax.ppermute only.
A program may use at most 320 MiB of HBM per device.

```python
import math
import jax
import jax.numpy as jnp
import numpy as np
from jax import lax

HEADS = 32
HEAD_DIM = 128
BLOCK = 128
WINDOW = 2048
NDOC = 8
SEGMENT_LENGTH = 2048
BLOCKS = 16
MOSTDOC = 8


def draw_log_gates(key, part):
    subkeys = jax.random.split(jax.random.fold_in(key, 11), 7)
    fast_share = 0.5
    fast_heads = jax.random.uniform(subkeys[0], (HEADS,)) < fast_share
    fast_rates = jnp.exp(jax.random.uniform(subkeys[1], (HEADS,), minval=jnp.log(1.0 / 50.0), maxval=jnp.log(1.0 / 30.0)))
    slow_rates = jax.random.uniform(subkeys[2], (HEADS,), minval=0.05, maxval=0.3) / SEGMENT_LENGTH
    base_rates = jnp.where(fast_heads, fast_rates, slow_rates)
    block_factor = jnp.exp(jax.random.uniform(subkeys[3], (SEGMENT_LENGTH // BLOCK, 1, HEADS), minval=jnp.log(0.6), maxval=jnp.log(1.8)))
    roughness = jax.random.uniform(subkeys[4], (SEGMENT_LENGTH // BLOCK, BLOCK, HEADS), minval=0.5, maxval=1.5)
    forgetting_factors = (base_rates * block_factor * roughness).reshape(SEGMENT_LENGTH, HEADS)
    slot_numbers = jax.random.randint(subkeys[5], (3,), 0, SEGMENT_LENGTH)
    objective_terms = jax.random.uniform(subkeys[6], (3, HEADS), minval=0.2, maxval=0.35)
    segment_ordinal = (jnp.arange(SEGMENT_LENGTH)[:, None] == slot_numbers[None, :]).astype(jnp.float32)
    segment_sequence = jnp.dot(segment_ordinal, jnp.log1p(-objective_terms))
    return (segment_sequence - forgetting_factors).astype(jnp.float32)


def paired(key):
    subkeys = jax.random.split(jax.random.fold_in(key, 23), 2)
    columns = HEADS * HEAD_DIM
    queries = jnp.clip(jax.random.normal(subkeys[0], (SEGMENT_LENGTH, columns)), -4.0, 4.0)
    key_rows = jnp.clip(jax.random.normal(subkeys[1], (SEGMENT_LENGTH, columns)), -4.0, 4.0)
    return (queries, key_rows)


def draw_attn_query(key, part):
    return paired(key)[0].astype(jnp.bfloat16)


def draw_attn_key(key, part):
    return paired(key)[1].astype(jnp.bfloat16)


def block_levels(stream_key, dims, cuts, least, largest):
    level, own = 1.0, jax.random.fold_in(stream_key, 6)
    for position, shards_of in cuts:
        draws = jnp.exp(jax.random.uniform(jax.random.fold_in(own, position), (shards_of,), jnp.float32, least / len(cuts), largest / len(cuts)))
        level = level * jnp.repeat(draws, dims[position] // shards_of).reshape([-1 if axis == position else 1 for axis in range(len(dims))])
    return level


def length_profile(count, total, most, slope):
    portions = [(1 << 20) // math.isqrt(standing ** slope) + 1 for standing in range(2, count + 1)]
    spare, counts = total - most - (count - 1), [1] * (count - 1)
    while spare > 0:
        movable = [i for i in range(count - 1) if counts[i] < most]
        mass, left = sum([portions[i] for i in movable]), spare
        for i in movable:
            addition = min(most - counts[i], max(1, left * portions[i] // mass), spare)
            counts[i] = counts[i] + addition
            spare = spare - addition
    return np.array([most] + counts)


def uneven(own_key, number_of, total, bound, lean):
    if number_of == 2:
        one = jax.random.randint(own_key, (), max(1, total - bound), min(bound, total - 1) + 1)
        return jnp.stack([one, total - one])
    lengths = jnp.asarray(length_profile(number_of, total, bound, lean), jnp.int32)
    couples = (number_of - 1) // 2
    giver, receiver = lengths[1:1 + 2 * couples:2], lengths[2:2 + 2 * couples:2]
    margin = jnp.minimum(giver - 1, bound - receiver)
    shifted = jax.random.randint(jax.random.fold_in(own_key, 1), (couples,), 0, 1 << 20) % (margin + 1)
    lengths = lengths.at[1:1 + 2 * couples:2].set(giver - shifted).at[2:2 + 2 * couples:2].set(receiver + shifted)
    return lengths[jax.random.permutation(jax.random.fold_in(own_key, 2), number_of)]


def gaussian(key, shape, spread, reach, shards=(), held_as=jnp.bfloat16):
    values = jax.random.normal(key, shape, jnp.float32) * spread
    if len(shards) > 0:
        values = block_levels(key, shape, shards, -0.22, 0.18) * values
    return jnp.clip(values, min=-reach, max=reach).astype(held_as)


def setup_inputs(seed: int = 0, part: int = 0) -> dict:
    seeds = jax.random.split(jax.random.key(seed), 9)
    own_keys = jax.random.split(jax.random.fold_in(seeds[8], part), 9)
    gla_query = gaussian(own_keys[0], (SEGMENT_LENGTH, HEADS * HEAD_DIM), 1.0, 6.0, ((0, 16),))
    gla_key = gaussian(own_keys[1], (SEGMENT_LENGTH, HEADS * HEAD_DIM), 1.0, 6.0, ((0, 16),))
    gla_value = gaussian(own_keys[2], (SEGMENT_LENGTH, HEADS * HEAD_DIM), 1.0, 6.0, ((0, 16),))
    log_gates = draw_log_gates(jax.random.fold_in(jax.random.fold_in(seeds[8], part), 71), part)
    norm_gain = jnp.clip(1.0 + 0.1 * jax.random.normal(seeds[4], (HEADS * HEAD_DIM,), jnp.float32), 0.5, 1.5)
    attn_query = draw_attn_query(jax.random.fold_in(jax.random.fold_in(seeds[8], part), 71), part)
    attn_key = draw_attn_key(jax.random.fold_in(jax.random.fold_in(seeds[8], part), 71), part)
    doc_blocks = uneven(own_keys[7], NDOC, BLOCKS, MOSTDOC, 2).astype(jnp.int32)
    return dict(gla_query=gla_query, gla_key=gla_key, gla_value=gla_value, log_gates=log_gates, norm_gain=norm_gain, attn_query=attn_query, attn_key=attn_key, doc_blocks=doc_blocks)


def doc_of_tokens(doc_blocks, total):
    doc_ends = jnp.cumsum(doc_blocks).astype(jnp.int32) * BLOCK
    positions = jnp.arange(total, dtype=jnp.int32)
    return lax.optimization_barrier(jnp.sum((positions[:, None] >= doc_ends[None, :]).astype(jnp.int32), axis=1)).astype(jnp.int32)

def gla_reference(gla_query, gla_key, gla_value, log_gates, norm_gain, doc_blocks):
    total = gla_query.shape[0]
    block_count = total // BLOCK
    doc_ends = jnp.cumsum(doc_blocks).astype(jnp.int32) * BLOCK
    starts = doc_ends - doc_blocks.astype(jnp.int32) * BLOCK
    block_offsets = jnp.arange(block_count, dtype=jnp.int32) * BLOCK
    resets = jnp.any(block_offsets[:, None] == starts[None, :], axis=1).astype(jnp.float32)
    shaped = (block_count, BLOCK, HEADS, HEAD_DIM)
    float_query = gla_query.reshape(shaped).astype(jnp.float32) * HEAD_DIM ** (-0.5)
    float_key = gla_key.reshape(shaped).astype(jnp.float32)
    float_value = gla_value.reshape(shaped).astype(jnp.float32)
    gate_sums = jnp.cumsum(log_gates.reshape(block_count, BLOCK, HEADS), axis=1)
    causal = jnp.arange(BLOCK)[:, None] >= jnp.arange(BLOCK)[None, :]

    def advance(carried, inputs):
        queries, key_rows, value_rows, summed, restart = inputs
        carried = carried * (1.0 - restart)
        block_last = summed[-1]
        by_head = summed.T
        gaps = by_head[:, :, None] - by_head[:, None, :]
        weight = jnp.where(causal[None], jnp.exp(jnp.where(causal[None], gaps, 0.0)), 0.0)
        scores = jnp.einsum('thd,shd->hts', queries, key_rows, precision=lax.Precision.HIGHEST) * weight
        inner_part = jnp.einsum('hts,shd->thd', scores, value_rows, precision=lax.Precision.HIGHEST)
        outer_part = jnp.einsum('thd,hde->the', queries * jnp.exp(summed)[..., None], carried, precision=lax.Precision.HIGHEST)
        tails = jnp.exp(block_last[None, :] - summed)
        updated = jnp.exp(block_last)[:, None, None] * carried + jnp.einsum('shd,she->hde', key_rows * tails[..., None], value_rows, precision=lax.Precision.HIGHEST)
        return (updated, inner_part + outer_part)
    initial = jnp.zeros((HEADS, HEAD_DIM, HEAD_DIM), jnp.float32)
    _, mixture = lax.scan(advance, initial, (float_query, float_key, float_value, gate_sums, resets))
    mean_square = lax.optimization_barrier(jnp.mean(mixture * mixture, axis=-1, keepdims=True))
    rescaled_hidden = mixture * lax.rsqrt(mean_square + 1e-06) * norm_gain.reshape(HEADS, HEAD_DIM)
    return rescaled_hidden.reshape(total, HEADS * HEAD_DIM).astype(jnp.bfloat16)

def attend_reference(queries, key_rows, value_rows, doc_ids):
    total = queries.shape[0]
    tile = min(512, total)

    def by_head(array):
        return array.reshape(total, HEADS, HEAD_DIM).transpose(1, 0, 2)
    pad_docs = jnp.concatenate([jnp.full((WINDOW,), -1, dtype=jnp.int32), doc_ids.astype(jnp.int32)])

    def one_head(operands):
        head_query, head_key, head_value = operands
        pad_key = jnp.concatenate([jnp.zeros((WINDOW, HEAD_DIM), head_key.dtype), head_key])
        pad_value = jnp.concatenate([jnp.zeros((WINDOW, HEAD_DIM), head_value.dtype), head_value])

        def one_tile(tile_index):
            tile_start = (tile_index * tile).astype(jnp.int32)
            tile_rows = lax.dynamic_slice_in_dim(head_query, tile_start, tile, 0)
            key_block = lax.dynamic_slice_in_dim(pad_key, tile_start, WINDOW + tile, 0)
            value_block = lax.dynamic_slice_in_dim(pad_value, tile_start, WINDOW + tile, 0)
            key_docs = lax.dynamic_slice_in_dim(pad_docs, tile_start, WINDOW + tile, 0)
            asker_documents = lax.dynamic_slice_in_dim(doc_ids.astype(jnp.int32), tile_start, tile, 0)
            query_pos = tile_start + jnp.arange(tile, dtype=jnp.int32)
            key_pos = tile_start - WINDOW + jnp.arange(WINDOW + tile, dtype=jnp.int32)
            allowed = (key_pos[None, :] <= query_pos[:, None]) & (key_pos[None, :] > query_pos[:, None] - WINDOW) & (key_docs[None, :] == asker_documents[:, None])
            scores = jnp.dot(tile_rows, key_block.T, preferred_element_type=jnp.float32) * HEAD_DIM ** (-0.5)
            scores = jnp.where(allowed, scores, -1e+30)
            row_peak = lax.optimization_barrier(jnp.max(scores, axis=-1, keepdims=True))
            exponent = jnp.exp(scores - row_peak)
            weights = (exponent / lax.optimization_barrier(jnp.sum(exponent, axis=-1, keepdims=True))).astype(jnp.bfloat16)
            return jnp.dot(weights, value_block, preferred_element_type=jnp.float32).astype(jnp.bfloat16)
        tiles_out = lax.map(one_tile, jnp.arange(total // tile, dtype=jnp.int32))
        return tiles_out.reshape(total, HEAD_DIM)
    result = lax.map(one_head, (by_head(queries), by_head(key_rows), by_head(value_rows)))
    return result.transpose(1, 0, 2).reshape(total, HEADS * HEAD_DIM)

def reference(gla_query, gla_key, gla_value, log_gates, norm_gain, attn_query, attn_key, doc_blocks):
    gla_mixed = gla_reference(gla_query, gla_key, gla_value, log_gates, norm_gain, doc_blocks)
    doc_ids = doc_of_tokens(doc_blocks, gla_query.shape[0])
    attended = attend_reference(attn_query, attn_key, gla_mixed, doc_ids)
    return (gla_mixed, attended)
```

```python
import functools

import jax
import jax.numpy as jnp
from jax import lax
from jax.experimental import pallas as pl
from jax.experimental.pallas import tpu as pltpu
from jax.sharding import PartitionSpec as P

BLOCK = 128
WINDOW = 2048
GATE_ROWS = 16


def entering_2(part, axis, combine, identity):
    place = lax.axis_index(axis)
    gathered = jax.tree.map(lambda a: lax.all_gather(a, axis), part)
    state = jax.tree.map(lambda a, e: jnp.zeros_like(a) + jnp.asarray(e, a.dtype), part, identity)

    def one(turn, state):
        return combine(
            state, jax.tree.map(lambda a: lax.dynamic_index_in_dim(a, turn, 0, False), gathered)
        )

    return lax.fori_loop(0, place, one, state)


def compose(earlier, later):
    return (earlier[0] * later[0], later[0][:, None, None] * earlier[1] + later[1])


def gla_layer(gla_query, gla_key, gla_value, log_gates, norm_gain, doc_blocks):
    tok_rows, columns = gla_query.shape
    head_count = log_gates.shape[1]
    head_dim = columns // head_count
    block_count = tok_rows // BLOCK
    offset = lax.axis_index("ctx") * tok_rows
    doc_ends = jnp.cumsum(doc_blocks) * BLOCK
    starts = doc_ends - doc_blocks * BLOCK
    block_offsets = offset + jnp.arange(block_count, dtype=jnp.int32) * BLOCK
    resets = jnp.any(block_offsets[:, None] == starts[None, :], axis=1).astype(jnp.float32)
    shaped = (block_count, BLOCK, head_count, head_dim)
    query_rows = gla_query.reshape(shaped)
    key_rows = gla_key.reshape(shaped)
    float_query = query_rows.astype(jnp.float32) * head_dim ** (-0.5)
    float_key = key_rows.astype(jnp.float32)
    float_value = gla_value.reshape(shaped).astype(jnp.float32)
    gate_sums = jnp.cumsum(log_gates.reshape(block_count, BLOCK, head_count), axis=1)
    block_last = gate_sums[:, -1, :]
    by_head = gate_sums.transpose(0, 2, 1)
    causal = (jnp.arange(BLOCK)[:, None] >= jnp.arange(BLOCK)[None, :])[None, None]
    gaps = by_head[:, :, :, None] - by_head[:, :, None, :]
    weight = jnp.where(causal, jnp.exp(jnp.where(causal, gaps, 0.0)), 0.0)
    raw_scores = jnp.einsum(
        "cthd,cshd->chts", query_rows, key_rows, preferred_element_type=jnp.float32
    )
    scores = raw_scores * head_dim ** (-0.5) * weight
    inner_part = jnp.einsum("chts,cshd->cthd", scores, float_value, precision=lax.Precision.HIGHEST)
    tails = jnp.exp(block_last[:, None, :] - gate_sums)
    local_state = jnp.einsum(
        "cshd,cshe->chde",
        float_key * tails[..., None],
        float_value,
        precision=lax.Precision.HIGHEST,
    )
    decays = jnp.exp(block_last) * (1.0 - resets)[:, None]
    total_decay = jnp.ones((head_count,), jnp.float32)
    total_state = jnp.zeros((head_count, head_dim, head_dim), jnp.float32)
    block_id = 0
    total_decay, total_state = compose(
        (total_decay, total_state), (decays[block_id], local_state[block_id])
    )
    identity = (
        jnp.ones((head_count,), jnp.float32),
        jnp.zeros((head_count, head_dim, head_dim), jnp.float32),
    )
    incoming = entering_2((total_decay, total_state), "ctx", compose, identity)
    carried = incoming[1]
    block_id = 0
    entering = carried * (1.0 - resets[block_id])
    scaled_query = float_query[block_id] * jnp.exp(gate_sums[block_id])[..., None]
    outer_parts = [
        jnp.einsum("thd,hde->the", scaled_query, entering, precision=lax.Precision.HIGHEST)
    ]
    mixture = inner_part + jnp.stack(outer_parts)
    mean_square = jnp.mean(mixture * mixture, axis=-1, keepdims=True)
    rescaled_hidden = (
        mixture * lax.rsqrt(mean_square + 1e-06) * norm_gain.reshape(head_count, head_dim)
    )
    return rescaled_hidden.reshape(tok_rows, columns).astype(jnp.bfloat16)


def attend(my_queries, query_places, key_rows, value_rows, doc_ids, span_factor):
    all_rows, unit_heads, head_dim = key_rows.shape
    length = my_queries.shape[0]
    tile = min(512, length)
    span = tile * span_factor
    pad_key = jnp.concatenate(
        [
            jnp.zeros((WINDOW, unit_heads, head_dim), jnp.bfloat16),
            key_rows,
            jnp.zeros((span, unit_heads, head_dim), jnp.bfloat16),
        ]
    )
    pad_value = jnp.concatenate(
        [
            jnp.zeros((WINDOW, unit_heads, head_dim), jnp.bfloat16),
            value_rows,
            jnp.zeros((span, unit_heads, head_dim), jnp.bfloat16),
        ]
    )
    pad_docs = jnp.concatenate(
        [jnp.full((WINDOW,), -1, dtype=jnp.int32), doc_ids, jnp.full((span,), -1, dtype=jnp.int32)]
    )

    def one_tile(tile_index):
        tile_rows = lax.dynamic_slice_in_dim(my_queries, tile_index * tile, tile, 0)
        query_pos = lax.dynamic_slice_in_dim(query_places, tile_index * tile, tile, 0)
        first_pos = query_pos[0]
        key_block = lax.dynamic_slice_in_dim(pad_key, first_pos, WINDOW + span, 0)
        value_block = lax.dynamic_slice_in_dim(pad_value, first_pos, WINDOW + span, 0)
        key_docs = lax.dynamic_slice_in_dim(pad_docs, first_pos, WINDOW + span, 0)
        asker_documents = jnp.take(doc_ids, query_pos)
        key_pos = first_pos - WINDOW + jnp.arange(WINDOW + span, dtype=jnp.int32)
        allowed = (
            (key_pos[None, :] <= query_pos[:, None])
            & (key_pos[None, :] > query_pos[:, None] - WINDOW)
            & (key_docs[None, :] == asker_documents[:, None])
        )
        scores = jnp.einsum(
            "qhd,khd->hqk", tile_rows, key_block, preferred_element_type=jnp.float32
        ) * head_dim ** (-0.5)
        scores = jnp.where(allowed[None], scores, -1e30)
        row_peak = jnp.max(scores, axis=-1, keepdims=True)
        exponent = jnp.exp(scores - row_peak)
        weights = (exponent / jnp.sum(exponent, axis=-1, keepdims=True)).astype(jnp.bfloat16)
        return jnp.einsum(
            "hqk,khd->qhd", weights, value_block, preferred_element_type=jnp.float32
        ).astype(jnp.bfloat16)

    tiles_out = lax.map(one_tile, jnp.arange(length // tile, dtype=jnp.int32))
    return tiles_out.reshape(length, unit_heads, head_dim)


def body(gla_query, gla_key, gla_value, log_gates, norm_gain, attn_query, attn_key, doc_blocks):
    tok_rows, columns = attn_query.shape
    head_count = log_gates.shape[1]
    head_dim = columns // head_count
    devices = lax.axis_size("ctx")
    copies = max(1, devices // head_count)
    per_unit = max(1, head_count // devices)
    groups = head_count // per_unit
    share_rows = tok_rows // copies

    def to_heads(rows_in):
        spread_rows = rows_in.reshape(tok_rows, head_count, 1, head_dim)
        spread_rows = jnp.broadcast_to(spread_rows, (tok_rows, head_count, copies, head_dim))
        return spread_rows.reshape(tok_rows, devices, per_unit * head_dim)

    shared = attn_query.reshape(copies, share_rows, groups, per_unit * head_dim).transpose(
        1, 2, 0, 3
    )
    sent_query = shared.reshape(share_rows, devices, per_unit * head_dim)
    gla_mixed = gla_layer(gla_query, gla_key, gla_value, log_gates, norm_gain, doc_blocks)
    moved_query, moved_key, moved_value = (
        lax.all_to_all(sent_query, "ctx", split_axis=1, concat_axis=0, tiled=True),
        lax.all_to_all(to_heads(attn_key), "ctx", split_axis=1, concat_axis=0, tiled=True),
        lax.all_to_all(to_heads(gla_mixed), "ctx", split_axis=1, concat_axis=0, tiled=True),
    )
    all_rows = devices * tok_rows
    unit_shape = (all_rows, per_unit, head_dim)
    moved_query = moved_query.reshape(-1, per_unit, head_dim)
    moved_key = moved_key.reshape(unit_shape)
    moved_value = moved_value.reshape(unit_shape)
    doc_ends = jnp.cumsum(doc_blocks) * BLOCK
    positions = jnp.arange(all_rows, dtype=jnp.int32)
    doc_ids = jnp.sum((positions[:, None] >= doc_ends[None, :]).astype(jnp.int32), axis=1)
    local_replica = lax.axis_index("ctx") % copies
    query_places = (
        jnp.arange(devices, dtype=jnp.int32)[:, None] * tok_rows
        + local_replica * share_rows
        + jnp.arange(share_rows, dtype=jnp.int32)[None, :]
    ).reshape(-1)
    result = attend(moved_query, query_places, moved_key, moved_value, doc_ids, copies)
    outgoing = result.reshape(devices, share_rows, 1, per_unit * head_dim)
    returned = lax.all_to_all(outgoing, "ctx", split_axis=0, concat_axis=2, tiled=True)
    regrouped = returned.reshape(share_rows, groups, copies, per_unit, head_dim).transpose(
        2, 0, 1, 3, 4
    )
    attended = regrouped.reshape(tok_rows, head_count, head_dim)
    return (gla_mixed, attended.reshape(tok_rows, columns))


def scalar_layout(docs, place, pieces):
    end, kind, index, start = jnp.int32(0), jnp.int32(0), jnp.int32(0), jnp.int32(0)
    for d in range(docs.shape[0]):
        length = docs[d]
        inside = (place >= end) & (place < end + length)
        found = jnp.where(length == pieces, 2, jnp.where(length == 2, 1, 0))
        kind = jnp.where(inside, found, kind)
        index = jnp.where(inside, place - end, index)
        start = jnp.where(inside, end, start)
        end = end + length
    return kind, index, start


def pack_body(pieces, docs, place, gq, gk, gv, aq, ak, gates, out, meta, sums):
    piece = pl.program_id(0)
    rows = gq.shape[0]
    heads = sums.shape[0]
    width = gq.shape[1]
    dim = width * pieces // heads

    @pl.when(piece == 0)
    def _():
        kind, index, start = scalar_layout(docs, place[0], pieces)
        alone = place[1] - pieces + 3
        meta[0] = jnp.where(kind == 2, start, jnp.where(kind == 1, alone - 2 + start % 2, alone))
        meta[1] = kind
        meta[2] = index
        meta[3] = start
        below = lax.broadcasted_iota(jnp.int32, (rows, rows), 0)
        until = lax.broadcasted_iota(jnp.int32, (rows, rows), 1)
        upper = (below <= until).astype(jnp.float32)
        sums[...] = lax.dot_general(
            gates[...],
            upper,
            (((0,), (0,)), ((), ())),
            precision=lax.Precision.HIGHEST,
            preferred_element_type=jnp.float32,
        )

    out[0, 0:rows] = gq[...]
    out[0, rows : 2 * rows] = gk[...]
    out[0, 2 * rows : 3 * rows] = gv[...]
    out[0, 3 * rows : 4 * rows] = aq[...]
    out[0, 4 * rows : 5 * rows] = ak[...]
    per = width // dim
    part = lax.broadcasted_iota(jnp.int32, (GATE_ROWS, rows), 0)
    for h in range(per):
        line = sums[pl.ds(piece * per + h, 1), :]
        first = line.astype(jnp.bfloat16).astype(jnp.float32)
        rest = line - first
        second = rest.astype(jnp.bfloat16).astype(jnp.float32)
        third = rest - second
        tile = jnp.where(part == 0, first, jnp.where(part == 1, second, jnp.where(part == 2, third, 0.0)))
        out[0, 5 * rows : 5 * rows + GATE_ROWS, h * dim : (h + 1) * dim] = tile.astype(jnp.bfloat16)


def pack(docs, place, gq, gk, gv, aq, ak, gates, pieces):
    rows, columns = gq.shape
    heads = gates.shape[1]
    width = columns // pieces
    tall = 5 * rows + GATE_ROWS
    wide = pl.BlockSpec((rows, width), lambda j: (0, j))
    small = pl.BlockSpec(memory_space=pltpu.SMEM)
    return pl.pallas_call(
        functools.partial(pack_body, pieces),
        grid=(pieces,),
        in_specs=[small, small] + [wide] * 5 + [pl.BlockSpec((rows, heads), lambda j: (0, 0))],
        out_specs=[pl.BlockSpec((1, tall, width), lambda j: (j, 0, 0)), small],
        out_shape=[
            jax.ShapeDtypeStruct((pieces, tall, width), jnp.bfloat16),
            jax.ShapeDtypeStruct((4,), jnp.int32),
        ],
        scratch_shapes=[pltpu.VMEM((heads, rows), jnp.float32)],
        name="pack",
    )(docs, place, gq, gk, gv, aq, ak, gates)


def halves(x):
    high = x.astype(jnp.bfloat16)
    return high, (x - high.astype(jnp.float32)).astype(jnp.bfloat16)


def mm(a, b):
    return jnp.dot(a, b, preferred_element_type=jnp.float32)


def mm_t(a, b):
    return lax.dot_general(a, b, (((1,), (1,)), ((), ())), preferred_element_type=jnp.float32)


def mix_body(meta, got, gain, out, values):
    pieces = got.shape[0]
    dim = got.shape[2]
    rows = values.shape[1]
    scale = dim ** (-0.5)
    kind, index = meta[1], meta[2]
    half = pieces // 2
    at, group, linked = [], [], []
    for n in range(pieces):
        slot = jnp.where(kind == 1, (n % 2) * half + n // 2, n)
        at.append(slot)
        group.append(jnp.where(kind == 2, index, jnp.where(kind == 1, half * index + n // 2, n)))
        linked.append((kind == 2) | ((kind == 1) & (n % 2 == 1)) if n else None)
    row = lax.broadcasted_iota(jnp.int32, (rows, rows), 0)
    col = lax.broadcasted_iota(jnp.int32, (rows, rows), 1)
    causal = row >= col
    state = None
    for n in range(pieces):
        slot = at[n]
        query = got[slot, 0:rows]
        key = got[slot, rows : 2 * rows]
        value = got[slot, 2 * rows : 3 * rows]
        line = jnp.sum(
            got[slot, 5 * rows : 5 * rows + GATE_ROWS].astype(jnp.float32), axis=0, keepdims=True
        )
        across = jnp.broadcast_to(line, (rows, rows))
        down = across.T
        last = down[rows - 1 : rows, :]
        weight = jnp.where(causal, jnp.exp(down - across), 0.0)
        inside = mm_t(query, key) * (weight * scale)
        inside_high, inside_low = halves(inside)
        mixture = mm(inside_high, value) + mm(inside_low, value)
        tail_high, tail_low = halves(key.astype(jnp.float32).T * jnp.exp(last - line))
        added = mm(tail_high, value) + mm(tail_low, value)
        if n:
            state = state * linked[n].astype(jnp.float32)
            state_high, state_low = halves(state)
            far_high, far_low = halves(query.astype(jnp.float32) * (jnp.exp(down) * scale))
            mixture = mixture + (
                mm(far_high, state_high) + mm(far_low, state_high) + mm(far_high, state_low)
            )
            state = state * jnp.exp(last) + added
        else:
            state = added
        square = jnp.mean(mixture * mixture, axis=-1, keepdims=True)
        mixed = mixture * lax.rsqrt(square + 1e-06) * gain[pl.ds(group[n], 1), :]
        mixed = mixed.astype(jnp.bfloat16)
        values[n] = mixed
        out[slot, 0:rows] = mixed
    for a in range(half):
        queries = jnp.concatenate([got[at[n], 3 * rows : 4 * rows] for n in (2 * a, 2 * a + 1)], axis=0)
        keys = jnp.concatenate([got[at[m], 4 * rows : 5 * rows] for m in range(2 * a + 2)], axis=0)
        scores = mm_t(queries, keys)
        whole = kind == 2
        parts = []
        if a:
            parts.append(scores[:, : 2 * a * rows] + jnp.where(whole, 0.0, -1e30))
        near = scores[:, 2 * a * rows :]
        open_ = jnp.where(kind == 0, -1e30, 0.0)
        upper = jnp.where(causal, near[:rows, :rows], -1e30)
        shut = jnp.full((rows, rows), -1e30, jnp.float32)
        lower = near[rows:, :rows] + open_
        right = jnp.where(causal, near[rows:, rows:], -1e30)
        parts.append(
            jnp.concatenate(
                [
                    jnp.concatenate([upper, shut], axis=1),
                    jnp.concatenate([lower, right], axis=1),
                ],
                axis=0,
            )
        )
        scores = jnp.concatenate(parts, axis=1) if a else parts[0]
        peak = jnp.max(scores, axis=-1, keepdims=True)
        exponent = jnp.exp((scores - peak) * scale)
        total = jnp.sum(exponent, axis=-1, keepdims=True)
        stacked = values[0 : 2 * a + 2].reshape((2 * a + 2) * rows, dim)
        result = (mm(exponent.astype(jnp.bfloat16), stacked) / total).astype(jnp.bfloat16)
        out[at[2 * a], rows : 2 * rows] = result[:rows]
        out[at[2 * a + 1], rows : 2 * rows] = result[rows:]


def mix(meta, got, norm_gain, rows, dim):
    pieces, tall, width = got.shape
    gain = norm_gain.reshape(pieces, width)
    return pl.pallas_call(
        mix_body,
        grid=(width // dim,),
        in_specs=[
            pl.BlockSpec(memory_space=pltpu.SMEM),
            pl.BlockSpec((pieces, tall, dim), lambda h: (0, 0, h)),
            pl.BlockSpec((pieces, dim), lambda h: (0, h)),
        ],
        out_specs=pl.BlockSpec((pieces, 2 * rows, dim), lambda h: (0, 0, h)),
        out_shape=jax.ShapeDtypeStruct((pieces, 2 * rows, width), jnp.bfloat16),
        scratch_shapes=[pltpu.VMEM((pieces, rows, dim), jnp.bfloat16)],
        name="mix",
    )(meta, got, gain)


def unpack_body(got, first, second):
    rows = first.shape[0]
    first[...] = got[0, :rows]
    second[...] = got[0, rows:]


def unpack(got, rows):
    pieces, tall, width = got.shape
    wide = pl.BlockSpec((rows, width), lambda j: (0, j))
    shape = jax.ShapeDtypeStruct((rows, pieces * width), jnp.bfloat16)
    return pl.pallas_call(
        unpack_body,
        grid=(pieces,),
        in_specs=[pl.BlockSpec((1, tall, width), lambda j: (j, 0, 0))],
        out_specs=[wide, wide],
        out_shape=[shape, shape],
        name="unpack",
    )(got)


def document_body(gla_query, gla_key, gla_value, log_gates, norm_gain, attn_query, attn_key, doc_blocks):
    rows, columns = attn_query.shape
    dim = columns // log_gates.shape[1]
    devices = lax.axis_size("ctx")
    pieces = devices // 2
    place = jnp.stack([lax.axis_index("ctx"), jnp.int32(devices)])
    sent, meta = pack(
        doc_blocks, place, gla_query, gla_key, gla_value, attn_query, attn_key, log_gates, pieces
    )
    members = []
    for start in range(devices - pieces + 1):
        inside = list(range(start, start + pieces))
        members.append([inside, [i for i in range(devices) if i not in inside]])
    for start in range(2):
        members.append([[(i + start) % devices, (i + start + 1) % devices] for i in range(0, devices, 2)])

    def exchange(groups):
        return lambda x: lax.all_to_all(
            x, "ctx", split_axis=0, concat_axis=0, tiled=True, axis_index_groups=groups
        )

    branches = [exchange(groups) for groups in members] + [lambda x: x]
    got = lax.switch(meta[0], branches, sent)
    mixed = mix(meta, got, norm_gain, rows, dim)
    back = lax.switch(meta[0], branches, mixed)
    return tuple(unpack(back, rows))


def solution(mesh):
    placed = (
        P(("grp", "ctx"), None),
        P(("grp", "ctx"), None),
        P(("grp", "ctx"), None),
        P(("grp", "ctx"), None),
        P(),
        P(("grp", "ctx"), None),
        P(("grp", "ctx"), None),
        P("grp"),
    )
    parts, devices = mesh.shape["grp"], mesh.shape["ctx"]

    def step(gla_query, gla_key, gla_value, log_gates, norm_gain, attn_query, attn_key, doc_blocks):
        blocks = gla_query.shape[0] // parts // BLOCK
        documents = doc_blocks.shape[0] // parts
        longest = blocks // 2
        spare = blocks - longest - (documents - 1)
        heads = log_gates.shape[1]
        simple = blocks == devices and spare == 1 and heads % longest == 0 and longest * BLOCK <= WINDOW
        simple = simple and longest > 2 and longest % 2 == 0
        return jax.shard_map(
            document_body if simple else body,
            mesh=mesh,
            in_specs=placed,
            out_specs=(P(("grp", "ctx"), None), P(("grp", "ctx"), None)),
            check_vma=False,
        )(gla_query, gla_key, gla_value, log_gates, norm_gain, attn_query, attn_key, doc_blocks)

    return step
```

```python
import functools

import jax
import jax.numpy as jnp
from jax import lax
from jax.experimental import pallas as pl
from jax.experimental.pallas import tpu as pltpu
from jax.sharding import PartitionSpec as P

BLOCK = 128
WINDOW = 2048
GATE_ROWS = 16
ROOM = 24 * 2**20


def entering_2(part, axis, combine, identity):
    place = lax.axis_index(axis)
    gathered = jax.tree.map(lambda a: lax.all_gather(a, axis), part)
    state = jax.tree.map(lambda a, e: jnp.zeros_like(a) + jnp.asarray(e, a.dtype), part, identity)

    def one(turn, state):
        return combine(
            state, jax.tree.map(lambda a: lax.dynamic_index_in_dim(a, turn, 0, False), gathered)
        )

    return lax.fori_loop(0, place, one, state)


def compose(earlier, later):
    return (earlier[0] * later[0], later[0][:, None, None] * earlier[1] + later[1])


def gla_layer(gla_query, gla_key, gla_value, log_gates, norm_gain, doc_blocks):
    tok_rows, columns = gla_query.shape
    head_count = log_gates.shape[1]
    head_dim = columns // head_count
    block_count = tok_rows // BLOCK
    offset = lax.axis_index("ctx") * tok_rows
    doc_ends = jnp.cumsum(doc_blocks) * BLOCK
    starts = doc_ends - doc_blocks * BLOCK
    block_offsets = offset + jnp.arange(block_count, dtype=jnp.int32) * BLOCK
    resets = jnp.any(block_offsets[:, None] == starts[None, :], axis=1).astype(jnp.float32)
    shaped = (block_count, BLOCK, head_count, head_dim)
    query_rows = gla_query.reshape(shaped)
    key_rows = gla_key.reshape(shaped)
    float_query = query_rows.astype(jnp.float32) * head_dim ** (-0.5)
    float_key = key_rows.astype(jnp.float32)
    float_value = gla_value.reshape(shaped).astype(jnp.float32)
    gate_sums = jnp.cumsum(log_gates.reshape(block_count, BLOCK, head_count), axis=1)
    block_last = gate_sums[:, -1, :]
    by_head = gate_sums.transpose(0, 2, 1)
    causal = (jnp.arange(BLOCK)[:, None] >= jnp.arange(BLOCK)[None, :])[None, None]
    gaps = by_head[:, :, :, None] - by_head[:, :, None, :]
    weight = jnp.where(causal, jnp.exp(jnp.where(causal, gaps, 0.0)), 0.0)
    raw_scores = jnp.einsum(
        "cthd,cshd->chts", query_rows, key_rows, preferred_element_type=jnp.float32
    )
    scores = raw_scores * head_dim ** (-0.5) * weight
    inner_part = jnp.einsum("chts,cshd->cthd", scores, float_value, precision=lax.Precision.HIGHEST)
    tails = jnp.exp(block_last[:, None, :] - gate_sums)
    local_state = jnp.einsum(
        "cshd,cshe->chde",
        float_key * tails[..., None],
        float_value,
        precision=lax.Precision.HIGHEST,
    )
    decays = jnp.exp(block_last) * (1.0 - resets)[:, None]
    total_decay = jnp.ones((head_count,), jnp.float32)
    total_state = jnp.zeros((head_count, head_dim, head_dim), jnp.float32)
    block_id = 0
    total_decay, total_state = compose(
        (total_decay, total_state), (decays[block_id], local_state[block_id])
    )
    identity = (
        jnp.ones((head_count,), jnp.float32),
        jnp.zeros((head_count, head_dim, head_dim), jnp.float32),
    )
    incoming = entering_2((total_decay, total_state), "ctx", compose, identity)
    carried = incoming[1]
    block_id = 0
    entering = carried * (1.0 - resets[block_id])
    scaled_query = float_query[block_id] * jnp.exp(gate_sums[block_id])[..., None]
    outer_parts = [
        jnp.einsum("thd,hde->the", scaled_query, entering, precision=lax.Precision.HIGHEST)
    ]
    mixture = inner_part + jnp.stack(outer_parts)
    mean_square = jnp.mean(mixture * mixture, axis=-1, keepdims=True)
    rescaled_hidden = (
        mixture * lax.rsqrt(mean_square + 1e-06) * norm_gain.reshape(head_count, head_dim)
    )
    return rescaled_hidden.reshape(tok_rows, columns).astype(jnp.bfloat16)


def attend(my_queries, query_places, key_rows, value_rows, doc_ids, span_factor):
    all_rows, unit_heads, head_dim = key_rows.shape
    length = my_queries.shape[0]
    tile = min(512, length)
    span = tile * span_factor
    pad_key = jnp.concatenate(
        [
            jnp.zeros((WINDOW, unit_heads, head_dim), jnp.bfloat16),
            key_rows,
            jnp.zeros((span, unit_heads, head_dim), jnp.bfloat16),
        ]
    )
    pad_value = jnp.concatenate(
        [
            jnp.zeros((WINDOW, unit_heads, head_dim), jnp.bfloat16),
            value_rows,
            jnp.zeros((span, unit_heads, head_dim), jnp.bfloat16),
        ]
    )
    pad_docs = jnp.concatenate(
        [jnp.full((WINDOW,), -1, dtype=jnp.int32), doc_ids, jnp.full((span,), -1, dtype=jnp.int32)]
    )

    def one_tile(tile_index):
        tile_rows = lax.dynamic_slice_in_dim(my_queries, tile_index * tile, tile, 0)
        query_pos = lax.dynamic_slice_in_dim(query_places, tile_index * tile, tile, 0)
        first_pos = query_pos[0]
        key_block = lax.dynamic_slice_in_dim(pad_key, first_pos, WINDOW + span, 0)
        value_block = lax.dynamic_slice_in_dim(pad_value, first_pos, WINDOW + span, 0)
        key_docs = lax.dynamic_slice_in_dim(pad_docs, first_pos, WINDOW + span, 0)
        asker_documents = jnp.take(doc_ids, query_pos)
        key_pos = first_pos - WINDOW + jnp.arange(WINDOW + span, dtype=jnp.int32)
        allowed = (
            (key_pos[None, :] <= query_pos[:, None])
            & (key_pos[None, :] > query_pos[:, None] - WINDOW)
            & (key_docs[None, :] == asker_documents[:, None])
        )
        scores = jnp.einsum(
            "qhd,khd->hqk", tile_rows, key_block, preferred_element_type=jnp.float32
        ) * head_dim ** (-0.5)
        scores = jnp.where(allowed[None], scores, -1e30)
        row_peak = jnp.max(scores, axis=-1, keepdims=True)
        exponent = jnp.exp(scores - row_peak)
        weights = (exponent / jnp.sum(exponent, axis=-1, keepdims=True)).astype(jnp.bfloat16)
        return jnp.einsum(
            "hqk,khd->qhd", weights, value_block, preferred_element_type=jnp.float32
        ).astype(jnp.bfloat16)

    tiles_out = lax.map(one_tile, jnp.arange(length // tile, dtype=jnp.int32))
    return tiles_out.reshape(length, unit_heads, head_dim)


def body(gla_query, gla_key, gla_value, log_gates, norm_gain, attn_query, attn_key, doc_blocks):
    tok_rows, columns = attn_query.shape
    head_count = log_gates.shape[1]
    head_dim = columns // head_count
    devices = lax.axis_size("ctx")
    copies = max(1, devices // head_count)
    per_unit = max(1, head_count // devices)
    groups = head_count // per_unit
    share_rows = tok_rows // copies

    def to_heads(rows_in):
        spread_rows = rows_in.reshape(tok_rows, head_count, 1, head_dim)
        spread_rows = jnp.broadcast_to(spread_rows, (tok_rows, head_count, copies, head_dim))
        return spread_rows.reshape(tok_rows, devices, per_unit * head_dim)

    shared = attn_query.reshape(copies, share_rows, groups, per_unit * head_dim).transpose(
        1, 2, 0, 3
    )
    sent_query = shared.reshape(share_rows, devices, per_unit * head_dim)
    gla_mixed = gla_layer(gla_query, gla_key, gla_value, log_gates, norm_gain, doc_blocks)
    moved_query, moved_key, moved_value = (
        lax.all_to_all(sent_query, "ctx", split_axis=1, concat_axis=0, tiled=True),
        lax.all_to_all(to_heads(attn_key), "ctx", split_axis=1, concat_axis=0, tiled=True),
        lax.all_to_all(to_heads(gla_mixed), "ctx", split_axis=1, concat_axis=0, tiled=True),
    )
    all_rows = devices * tok_rows
    unit_shape = (all_rows, per_unit, head_dim)
    moved_query = moved_query.reshape(-1, per_unit, head_dim)
    moved_key = moved_key.reshape(unit_shape)
    moved_value = moved_value.reshape(unit_shape)
    doc_ends = jnp.cumsum(doc_blocks) * BLOCK
    positions = jnp.arange(all_rows, dtype=jnp.int32)
    doc_ids = jnp.sum((positions[:, None] >= doc_ends[None, :]).astype(jnp.int32), axis=1)
    local_replica = lax.axis_index("ctx") % copies
    query_places = (
        jnp.arange(devices, dtype=jnp.int32)[:, None] * tok_rows
        + local_replica * share_rows
        + jnp.arange(share_rows, dtype=jnp.int32)[None, :]
    ).reshape(-1)
    result = attend(moved_query, query_places, moved_key, moved_value, doc_ids, copies)
    outgoing = result.reshape(devices, share_rows, 1, per_unit * head_dim)
    returned = lax.all_to_all(outgoing, "ctx", split_axis=0, concat_axis=2, tiled=True)
    regrouped = returned.reshape(share_rows, groups, copies, per_unit, head_dim).transpose(
        2, 0, 1, 3, 4
    )
    attended = regrouped.reshape(tok_rows, head_count, head_dim)
    return (gla_mixed, attended.reshape(tok_rows, columns))


def scalar_layout(docs, place, pieces):
    end, kind, index, start = jnp.int32(0), jnp.int32(0), jnp.int32(0), jnp.int32(0)
    for d in range(docs.shape[0]):
        length = docs[d]
        inside = (place >= end) & (place < end + length)
        found = jnp.where(length == pieces, 2, jnp.where(length == 2, 1, 0))
        kind = jnp.where(inside, found, kind)
        index = jnp.where(inside, place - end, index)
        start = jnp.where(inside, end, start)
        end = end + length
    return kind, index, start


def place_body(docs, meta):
    pieces = lax.axis_size("ctx") // 2
    kind, index, start = scalar_layout(docs, lax.axis_index("ctx"), pieces)
    alone = lax.axis_size("ctx") - pieces + 3
    meta[0] = jnp.where(kind == 2, start, jnp.where(kind == 1, alone - 2 + start % 2, alone))
    meta[1] = kind
    meta[2] = index
    meta[3] = start


def find_place(docs):
    small = pl.BlockSpec(memory_space=pltpu.SMEM)
    return pl.pallas_call(
        place_body,
        in_specs=[small],
        out_specs=small,
        out_shape=jax.ShapeDtypeStruct((4,), jnp.int32),
        name="place",
    )(docs)


def pack_body(gq, gk, gv, aq, ak, gates, out):
    pieces, per, _, dim = out.shape
    rows = gq.shape[0]
    below = lax.broadcasted_iota(jnp.int32, (rows, rows), 0)
    until = lax.broadcasted_iota(jnp.int32, (rows, rows), 1)
    sums = jnp.dot(
        gates[...],
        (below <= until).astype(jnp.float32),
        precision=lax.Precision.HIGHEST,
        preferred_element_type=jnp.float32,
    )
    part = lax.broadcasted_iota(jnp.int32, (GATE_ROWS, rows), 0)
    for head in range(pieces * per):
        line = sums[head : head + 1, :]
        first = line.astype(jnp.bfloat16).astype(jnp.float32)
        rest = line - first
        second = rest.astype(jnp.bfloat16).astype(jnp.float32)
        third = rest - second
        tile = jnp.where(part == 0, first, jnp.where(part == 1, second, jnp.where(part == 2, third, 0.0)))
        out[head // per, head % per, 5 * rows :] = tile.astype(jnp.bfloat16)
    for i, source in enumerate((gq, gk, gv, aq, ak)):
        for head in range(pieces * per):
            out[head // per, head % per, i * rows : (i + 1) * rows] = source[
                :, head * dim : (head + 1) * dim
            ]


def pack(gq, gk, gv, aq, ak, gates):
    rows, columns = gq.shape
    heads = gates.shape[0]
    pieces = lax.axis_size("ctx") // 2
    whole = pl.BlockSpec(memory_space=pltpu.VMEM)
    return pl.pallas_call(
        pack_body,
        in_specs=[whole] * 6,
        out_specs=whole,
        out_shape=jax.ShapeDtypeStruct(
            (pieces, heads // pieces, 5 * rows + GATE_ROWS, columns // heads), jnp.bfloat16
        ),
        compiler_params=pltpu.CompilerParams(vmem_limit_bytes=ROOM),
        name="pack",
    )(gq, gk, gv, aq, ak, gates)


def halves(x):
    high = x.astype(jnp.bfloat16)
    return high, (x - high.astype(jnp.float32)).astype(jnp.bfloat16)


def mm(a, b):
    return jnp.dot(a, b, preferred_element_type=jnp.float32)


def mm_t(a, b):
    return lax.dot_general(a, b, (((1,), (1,)), ((), ())), preferred_element_type=jnp.float32)


def mix_body(meta, got, gain, out, values):
    mix_head(meta, got.at[:, 0], gain.at[0], out.at[:, 0], values)


def mix_head(meta, got, gain, out, values):
    pieces, _, dim = got.shape
    rows = values.shape[1]
    scale = dim ** (-0.5)
    kind, index = meta[1], meta[2]
    half = pieces // 2
    at, group, linked = [], [], []
    for n in range(pieces):
        slot = jnp.where(kind == 1, (n % 2) * half + n // 2, n)
        at.append(slot)
        group.append(jnp.where(kind == 2, index, jnp.where(kind == 1, half * index + n // 2, n)))
        linked.append((kind == 2) | ((kind == 1) & (n % 2 == 1)) if n else None)
    row = lax.broadcasted_iota(jnp.int32, (rows, rows), 0)
    col = lax.broadcasted_iota(jnp.int32, (rows, rows), 1)
    causal = row >= col
    state = None
    for n in range(pieces):
        slot = at[n]
        query = got[slot, 0:rows]
        key = got[slot, rows : 2 * rows]
        value = got[slot, 2 * rows : 3 * rows]
        line = jnp.sum(
            got[slot, 5 * rows : 5 * rows + GATE_ROWS].astype(jnp.float32), axis=0, keepdims=True
        )
        across = jnp.broadcast_to(line, (rows, rows))
        down = across.T
        last = down[rows - 1 : rows, :]
        weight = jnp.where(causal, jnp.exp(down - across), 0.0)
        inside = mm_t(query, key) * (weight * scale)
        inside_high, inside_low = halves(inside)
        mixture = mm(inside_high, value) + mm(inside_low, value)
        tail_high, tail_low = halves(key.astype(jnp.float32).T * jnp.exp(last - line))
        added = mm(tail_high, value) + mm(tail_low, value)
        if n:
            state = state * linked[n].astype(jnp.float32)
            state_high, state_low = halves(state)
            far_high, far_low = halves(query.astype(jnp.float32) * (jnp.exp(down) * scale))
            mixture = mixture + (
                mm(far_high, state_high) + mm(far_low, state_high) + mm(far_high, state_low)
            )
            state = state * jnp.exp(last) + added
        else:
            state = added
        square = jnp.mean(mixture * mixture, axis=-1, keepdims=True)
        mixed = mixture * lax.rsqrt(square + 1e-06) * gain[pl.ds(group[n], 1), :]
        mixed = mixed.astype(jnp.bfloat16)
        values[n] = mixed
        out[slot, 0:rows] = mixed
    for a in range(half):
        queries = jnp.concatenate([got[at[n], 3 * rows : 4 * rows] for n in (2 * a, 2 * a + 1)], axis=0)
        keys = jnp.concatenate([got[at[m], 4 * rows : 5 * rows] for m in range(2 * a + 2)], axis=0)
        scores = mm_t(queries, keys)
        whole = kind == 2
        parts = []
        if a:
            parts.append(scores[:, : 2 * a * rows] + jnp.where(whole, 0.0, -1e30))
        near = scores[:, 2 * a * rows :]
        open_ = jnp.where(kind == 0, -1e30, 0.0)
        upper = jnp.where(causal, near[:rows, :rows], -1e30)
        shut = jnp.full((rows, rows), -1e30, jnp.float32)
        lower = near[rows:, :rows] + open_
        right = jnp.where(causal, near[rows:, rows:], -1e30)
        parts.append(
            jnp.concatenate(
                [
                    jnp.concatenate([upper, shut], axis=1),
                    jnp.concatenate([lower, right], axis=1),
                ],
                axis=0,
            )
        )
        scores = jnp.concatenate(parts, axis=1) if a else parts[0]
        peak = jnp.max(scores, axis=-1, keepdims=True)
        exponent = jnp.exp((scores - peak) * scale)
        total = jnp.sum(exponent, axis=-1, keepdims=True)
        stacked = values[0 : 2 * a + 2].reshape((2 * a + 2) * rows, dim)
        result = (mm(exponent.astype(jnp.bfloat16), stacked) / total).astype(jnp.bfloat16)
        out[at[2 * a], rows : 2 * rows] = result[:rows]
        out[at[2 * a + 1], rows : 2 * rows] = result[rows:]


def mix(meta, got, norm_gain):
    pieces, per, tall, dim = got.shape
    rows = (tall - GATE_ROWS) // 5
    gain = norm_gain.reshape(pieces, per, dim).transpose(1, 0, 2)
    return pl.pallas_call(
        mix_body,
        grid=(per,),
        in_specs=[
            pl.BlockSpec(memory_space=pltpu.SMEM),
            pl.BlockSpec((pieces, 1, tall, dim), lambda h: (0, h, 0, 0)),
            pl.BlockSpec((1, pieces, dim), lambda h: (h, 0, 0)),
        ],
        out_specs=pl.BlockSpec((pieces, 1, 2 * rows, dim), lambda h: (0, h, 0, 0)),
        out_shape=jax.ShapeDtypeStruct((pieces, per, 2 * rows, dim), jnp.bfloat16),
        scratch_shapes=[pltpu.VMEM((pieces, rows, dim), jnp.bfloat16)],
        compiler_params=pltpu.CompilerParams(vmem_limit_bytes=ROOM),
        name="mix",
    )(meta, got, gain)


def unpack_body(got, first, second):
    pieces, per, tall, dim = got.shape
    for head in range(pieces * per):
        columns = slice(head * dim, (head + 1) * dim)
        first[:, columns] = got[head // per, head % per, : tall // 2]
        second[:, columns] = got[head // per, head % per, tall // 2 :]


def unpack(got):
    pieces, per, tall, dim = got.shape
    whole = pl.BlockSpec(memory_space=pltpu.VMEM)
    shape = jax.ShapeDtypeStruct((tall // 2, pieces * per * dim), jnp.bfloat16)
    return pl.pallas_call(
        unpack_body,
        in_specs=[whole],
        out_specs=[whole, whole],
        out_shape=[shape, shape],
        compiler_params=pltpu.CompilerParams(vmem_limit_bytes=ROOM),
        name="unpack",
    )(got)


def document_body(gla_query, gla_key, gla_value, log_gates, norm_gain, attn_query, attn_key, doc_blocks):
    devices = lax.axis_size("ctx")
    pieces = devices // 2
    meta = find_place(doc_blocks)
    held = (gla_query, gla_key, gla_value, attn_query, attn_key, log_gates.T)
    members = []
    for start in range(devices - pieces + 1):
        inside = list(range(start, start + pieces))
        members.append([inside, [i for i in range(devices) if i not in inside]])
    for start in range(2):
        members.append([[(i + start) % devices, (i + start + 1) % devices] for i in range(0, devices, 2)])

    def exchange(x, groups):
        return lax.all_to_all(x, "ctx", split_axis=0, concat_axis=0, tiled=True, axis_index_groups=groups)

    def outward(groups):
        return lambda *held: exchange(pack(*held), groups)

    def homeward(groups):
        return lambda x: exchange(x, groups)

    got = lax.switch(meta[0], [outward(groups) for groups in members] + [pack], *held)
    mixed = mix(meta, got, norm_gain)
    back = lax.switch(meta[0], [homeward(groups) for groups in members] + [lambda x: x], mixed)
    return tuple(unpack(back))


def solution(mesh):
    placed = (
        P(("grp", "ctx"), None),
        P(("grp", "ctx"), None),
        P(("grp", "ctx"), None),
        P(("grp", "ctx"), None),
        P(),
        P(("grp", "ctx"), None),
        P(("grp", "ctx"), None),
        P("grp"),
    )
    parts, devices = mesh.shape["grp"], mesh.shape["ctx"]

    def step(gla_query, gla_key, gla_value, log_gates, norm_gain, attn_query, attn_key, doc_blocks):
        blocks = gla_query.shape[0] // parts // BLOCK
        documents = doc_blocks.shape[0] // parts
        longest = blocks // 2
        spare = blocks - longest - (documents - 1)
        heads = log_gates.shape[1]
        simple = blocks == devices and spare == 1 and heads % longest == 0 and longest * BLOCK <= WINDOW
        simple = simple and longest > 2 and longest % 2 == 0
        return jax.shard_map(
            document_body if simple else body,
            mesh=mesh,
            in_specs=placed,
            out_specs=(P(("grp", "ctx"), None), P(("grp", "ctx"), None)),
            check_vma=False,
        )(gla_query, gla_key, gla_value, log_gates, norm_gain, attn_query, attn_key, doc_blocks)

    return step
```

```python
import functools

import jax
import jax.numpy as jnp
from jax import lax
from jax.experimental import pallas as pl
from jax.experimental.pallas import tpu as pltpu
from jax.sharding import PartitionSpec as P

BLOCK = 128
WINDOW = 2048
GATE_ROWS = 8
LOG2E = 1.4426950408889634
ROOM = 24 * 2**20


def entering_2(part, axis, combine, identity):
    place = lax.axis_index(axis)
    gathered = jax.tree.map(lambda a: lax.all_gather(a, axis), part)
    state = jax.tree.map(lambda a, e: jnp.zeros_like(a) + jnp.asarray(e, a.dtype), part, identity)

    def one(turn, state):
        return combine(
            state, jax.tree.map(lambda a: lax.dynamic_index_in_dim(a, turn, 0, False), gathered)
        )

    return lax.fori_loop(0, place, one, state)


def compose(earlier, later):
    return (earlier[0] * later[0], later[0][:, None, None] * earlier[1] + later[1])


def gla_layer(gla_query, gla_key, gla_value, log_gates, norm_gain, doc_blocks):
    tok_rows, columns = gla_query.shape
    head_count = log_gates.shape[1]
    head_dim = columns // head_count
    block_count = tok_rows // BLOCK
    offset = lax.axis_index("ctx") * tok_rows
    doc_ends = jnp.cumsum(doc_blocks) * BLOCK
    starts = doc_ends - doc_blocks * BLOCK
    block_offsets = offset + jnp.arange(block_count, dtype=jnp.int32) * BLOCK
    resets = jnp.any(block_offsets[:, None] == starts[None, :], axis=1).astype(jnp.float32)
    shaped = (block_count, BLOCK, head_count, head_dim)
    query_rows = gla_query.reshape(shaped)
    key_rows = gla_key.reshape(shaped)
    float_query = query_rows.astype(jnp.float32) * head_dim ** (-0.5)
    float_key = key_rows.astype(jnp.float32)
    float_value = gla_value.reshape(shaped).astype(jnp.float32)
    gate_sums = jnp.cumsum(log_gates.reshape(block_count, BLOCK, head_count), axis=1)
    block_last = gate_sums[:, -1, :]
    by_head = gate_sums.transpose(0, 2, 1)
    causal = (jnp.arange(BLOCK)[:, None] >= jnp.arange(BLOCK)[None, :])[None, None]
    gaps = by_head[:, :, :, None] - by_head[:, :, None, :]
    weight = jnp.where(causal, jnp.exp(jnp.where(causal, gaps, 0.0)), 0.0)
    raw_scores = jnp.einsum(
        "cthd,cshd->chts", query_rows, key_rows, preferred_element_type=jnp.float32
    )
    scores = raw_scores * head_dim ** (-0.5) * weight
    inner_part = jnp.einsum("chts,cshd->cthd", scores, float_value, precision=lax.Precision.HIGHEST)
    tails = jnp.exp(block_last[:, None, :] - gate_sums)
    local_state = jnp.einsum(
        "cshd,cshe->chde",
        float_key * tails[..., None],
        float_value,
        precision=lax.Precision.HIGHEST,
    )
    decays = jnp.exp(block_last) * (1.0 - resets)[:, None]
    total_decay = jnp.ones((head_count,), jnp.float32)
    total_state = jnp.zeros((head_count, head_dim, head_dim), jnp.float32)
    block_id = 0
    total_decay, total_state = compose(
        (total_decay, total_state), (decays[block_id], local_state[block_id])
    )
    identity = (
        jnp.ones((head_count,), jnp.float32),
        jnp.zeros((head_count, head_dim, head_dim), jnp.float32),
    )
    incoming = entering_2((total_decay, total_state), "ctx", compose, identity)
    carried = incoming[1]
    block_id = 0
    entering = carried * (1.0 - resets[block_id])
    scaled_query = float_query[block_id] * jnp.exp(gate_sums[block_id])[..., None]
    outer_parts = [
        jnp.einsum("thd,hde->the", scaled_query, entering, precision=lax.Precision.HIGHEST)
    ]
    mixture = inner_part + jnp.stack(outer_parts)
    mean_square = jnp.mean(mixture * mixture, axis=-1, keepdims=True)
    rescaled_hidden = (
        mixture * lax.rsqrt(mean_square + 1e-06) * norm_gain.reshape(head_count, head_dim)
    )
    return rescaled_hidden.reshape(tok_rows, columns).astype(jnp.bfloat16)


def attend(my_queries, query_places, key_rows, value_rows, doc_ids, span_factor):
    all_rows, unit_heads, head_dim = key_rows.shape
    length = my_queries.shape[0]
    tile = min(512, length)
    span = tile * span_factor
    pad_key = jnp.concatenate(
        [
            jnp.zeros((WINDOW, unit_heads, head_dim), jnp.bfloat16),
            key_rows,
            jnp.zeros((span, unit_heads, head_dim), jnp.bfloat16),
        ]
    )
    pad_value = jnp.concatenate(
        [
            jnp.zeros((WINDOW, unit_heads, head_dim), jnp.bfloat16),
            value_rows,
            jnp.zeros((span, unit_heads, head_dim), jnp.bfloat16),
        ]
    )
    pad_docs = jnp.concatenate(
        [jnp.full((WINDOW,), -1, dtype=jnp.int32), doc_ids, jnp.full((span,), -1, dtype=jnp.int32)]
    )

    def one_tile(tile_index):
        tile_rows = lax.dynamic_slice_in_dim(my_queries, tile_index * tile, tile, 0)
        query_pos = lax.dynamic_slice_in_dim(query_places, tile_index * tile, tile, 0)
        first_pos = query_pos[0]
        key_block = lax.dynamic_slice_in_dim(pad_key, first_pos, WINDOW + span, 0)
        value_block = lax.dynamic_slice_in_dim(pad_value, first_pos, WINDOW + span, 0)
        key_docs = lax.dynamic_slice_in_dim(pad_docs, first_pos, WINDOW + span, 0)
        asker_documents = jnp.take(doc_ids, query_pos)
        key_pos = first_pos - WINDOW + jnp.arange(WINDOW + span, dtype=jnp.int32)
        allowed = (
            (key_pos[None, :] <= query_pos[:, None])
            & (key_pos[None, :] > query_pos[:, None] - WINDOW)
            & (key_docs[None, :] == asker_documents[:, None])
        )
        scores = jnp.einsum(
            "qhd,khd->hqk", tile_rows, key_block, preferred_element_type=jnp.float32
        ) * head_dim ** (-0.5)
        scores = jnp.where(allowed[None], scores, -1e30)
        row_peak = jnp.max(scores, axis=-1, keepdims=True)
        exponent = jnp.exp(scores - row_peak)
        weights = (exponent / jnp.sum(exponent, axis=-1, keepdims=True)).astype(jnp.bfloat16)
        return jnp.einsum(
            "hqk,khd->qhd", weights, value_block, preferred_element_type=jnp.float32
        ).astype(jnp.bfloat16)

    tiles_out = lax.map(one_tile, jnp.arange(length // tile, dtype=jnp.int32))
    return tiles_out.reshape(length, unit_heads, head_dim)


def body(gla_query, gla_key, gla_value, log_gates, norm_gain, attn_query, attn_key, doc_blocks):
    tok_rows, columns = attn_query.shape
    head_count = log_gates.shape[1]
    head_dim = columns // head_count
    devices = lax.axis_size("ctx")
    copies = max(1, devices // head_count)
    per_unit = max(1, head_count // devices)
    groups = head_count // per_unit
    share_rows = tok_rows // copies

    def to_heads(rows_in):
        spread_rows = rows_in.reshape(tok_rows, head_count, 1, head_dim)
        spread_rows = jnp.broadcast_to(spread_rows, (tok_rows, head_count, copies, head_dim))
        return spread_rows.reshape(tok_rows, devices, per_unit * head_dim)

    shared = attn_query.reshape(copies, share_rows, groups, per_unit * head_dim).transpose(
        1, 2, 0, 3
    )
    sent_query = shared.reshape(share_rows, devices, per_unit * head_dim)
    gla_mixed = gla_layer(gla_query, gla_key, gla_value, log_gates, norm_gain, doc_blocks)
    moved_query, moved_key, moved_value = (
        lax.all_to_all(sent_query, "ctx", split_axis=1, concat_axis=0, tiled=True),
        lax.all_to_all(to_heads(attn_key), "ctx", split_axis=1, concat_axis=0, tiled=True),
        lax.all_to_all(to_heads(gla_mixed), "ctx", split_axis=1, concat_axis=0, tiled=True),
    )
    all_rows = devices * tok_rows
    unit_shape = (all_rows, per_unit, head_dim)
    moved_query = moved_query.reshape(-1, per_unit, head_dim)
    moved_key = moved_key.reshape(unit_shape)
    moved_value = moved_value.reshape(unit_shape)
    doc_ends = jnp.cumsum(doc_blocks) * BLOCK
    positions = jnp.arange(all_rows, dtype=jnp.int32)
    doc_ids = jnp.sum((positions[:, None] >= doc_ends[None, :]).astype(jnp.int32), axis=1)
    local_replica = lax.axis_index("ctx") % copies
    query_places = (
        jnp.arange(devices, dtype=jnp.int32)[:, None] * tok_rows
        + local_replica * share_rows
        + jnp.arange(share_rows, dtype=jnp.int32)[None, :]
    ).reshape(-1)
    result = attend(moved_query, query_places, moved_key, moved_value, doc_ids, copies)
    outgoing = result.reshape(devices, share_rows, 1, per_unit * head_dim)
    returned = lax.all_to_all(outgoing, "ctx", split_axis=0, concat_axis=2, tiled=True)
    regrouped = returned.reshape(share_rows, groups, copies, per_unit, head_dim).transpose(
        2, 0, 1, 3, 4
    )
    attended = regrouped.reshape(tok_rows, head_count, head_dim)
    return (gla_mixed, attended.reshape(tok_rows, columns))


def scalar_layout(docs, place, pieces):
    end, kind, index, start = jnp.int32(0), jnp.int32(0), jnp.int32(0), jnp.int32(0)
    for d in range(docs.shape[0]):
        length = docs[d]
        inside = (place >= end) & (place < end + length)
        found = jnp.where(length == pieces, 2, jnp.where(length == 2, 1, 0))
        kind = jnp.where(inside, found, kind)
        index = jnp.where(inside, place - end, index)
        start = jnp.where(inside, end, start)
        end = end + length
    return kind, index, start


def place_body(docs, meta):
    pieces = lax.axis_size("ctx") // 2
    kind, index, start = scalar_layout(docs, lax.axis_index("ctx"), pieces)
    alone = lax.axis_size("ctx") - pieces + 3
    meta[0] = jnp.where(kind == 2, start, jnp.where(kind == 1, alone - 2 + start % 2, alone))
    meta[1] = kind
    meta[2] = index
    meta[3] = start


def find_place(docs):
    small = pl.BlockSpec(memory_space=pltpu.SMEM)
    return pl.pallas_call(
        place_body,
        in_specs=[small],
        out_specs=small,
        out_shape=jax.ShapeDtypeStruct((4,), jnp.int32),
        name="place",
    )(docs)


def pack_body(gq, gk, gv, aq, ak, gates, out):
    pieces, per, _, dim = out.shape
    rows = gq.shape[0]
    below = lax.broadcasted_iota(jnp.int32, (rows, rows), 0)
    until = lax.broadcasted_iota(jnp.int32, (rows, rows), 1)
    sums = jnp.dot(
        gates[...],
        (below <= until).astype(jnp.float32),
        precision=lax.Precision.HIGHEST,
        preferred_element_type=jnp.float32,
    )
    part = lax.broadcasted_iota(jnp.int32, (GATE_ROWS, rows), 0)
    for head in range(pieces * per):
        line = sums[head : head + 1, :] * LOG2E
        first = line.astype(jnp.bfloat16).astype(jnp.float32)
        rest = line - first
        second = rest.astype(jnp.bfloat16).astype(jnp.float32)
        third = rest - second
        tile = jnp.where(part == 0, first, jnp.where(part == 1, second, jnp.where(part == 2, third, 0.0)))
        out[head // per, head % per, 5 * rows :] = tile.astype(jnp.bfloat16)

    def piece(j, carry):
        for i, source in enumerate((gq, gk, gv, aq, ak)):
            for h in range(per):
                columns = pl.ds(pl.multiple_of((j * per + h) * dim, dim), dim)
                out[j, h, i * rows : (i + 1) * rows] = source[:, columns]
        return carry

    lax.fori_loop(0, pieces, piece, 0)


def pack(gq, gk, gv, aq, ak, gates):
    rows, columns = gq.shape
    heads = gates.shape[0]
    pieces = lax.axis_size("ctx") // 2
    whole = pl.BlockSpec(memory_space=pltpu.VMEM)
    return pl.pallas_call(
        pack_body,
        in_specs=[whole] * 6,
        out_specs=whole,
        out_shape=jax.ShapeDtypeStruct(
            (pieces, heads // pieces, 5 * rows + GATE_ROWS, columns // heads), jnp.bfloat16
        ),
        compiler_params=pltpu.CompilerParams(vmem_limit_bytes=ROOM),
        name="pack",
    )(gq, gk, gv, aq, ak, gates)


def mm(a, b):
    return jnp.dot(a, b, preferred_element_type=jnp.float32)


def mm_t(a, b):
    return lax.dot_general(a, b, (((1,), (1,)), ((), ())), preferred_element_type=jnp.float32)


def mix_body(meta, got, gain, out, values):
    pieces, _, _, dim = got.shape
    rows = values.shape[2]
    kind, index = meta[1], meta[2]
    half = pieces // 2
    at, group = [], []
    for n in range(pieces):
        slot = jnp.where(kind == 1, (n % 2) * half + n // 2, n)
        at.append(slot)
        group.append(jnp.where(kind == 2, index, jnp.where(kind == 1, half * index + n // 2, n)))

    heads = range(got.shape[1])

    def part(h, n, i):
        return got[at[n], h, i * rows : (i + 1) * rows]

    row = lax.broadcasted_iota(jnp.int32, (2 * rows, 2 * rows), 0)
    col = lax.broadcasted_iota(jnp.int32, (2 * rows, 2 * rows), 1)
    wide = row >= col
    causal = wide[:rows, :rows]

    def recur(h, n, state, keep):
        query, key, value = part(h, n, 0), part(h, n, 1), part(h, n, 2)
        line = jnp.sum(got[at[n], h, 5 * rows :].astype(jnp.float32), axis=0, keepdims=True)
        across = jnp.broadcast_to(line, (rows, rows))
        down = across.T
        last = down[rows - 1 : rows, :]
        weight = jnp.where(causal, jnp.exp2(down - across), 0.0)
        mixture = mm((mm_t(query, key) * weight).astype(jnp.bfloat16), value)
        tail = (key.astype(jnp.float32).T * jnp.exp2(last - line)).astype(jnp.bfloat16)
        added = mm(tail, value)
        if state is not None:
            if keep is not None:
                state = state * keep
            far = (query.astype(jnp.float32) * jnp.exp2(down)).astype(jnp.bfloat16)
            mixture = mixture + mm(far, state.astype(jnp.bfloat16))
            added = state * jnp.exp2(last) + added
        square = jnp.mean(mixture * mixture, axis=-1, keepdims=True)
        mixed = mixture * lax.rsqrt(square + 1e-06 * dim) * gain[h, pl.ds(group[n], 1), :]
        mixed = mixed.astype(jnp.bfloat16)
        values[h, n] = mixed
        out[at[n], h, :rows] = mixed
        return added

    def attend_pair(h, first, n, open_):
        queries = jnp.concatenate([part(h, n - 1, 3), part(h, n, 3)], axis=0)
        keys = jnp.concatenate([part(h, m, 4) for m in range(first, n + 1)], axis=0)
        scores = mm_t(queries, keys)
        edge = (n - 1 - first) * rows
        near = jnp.where(open_, scores[:, edge:], -1e30)
        scores = jnp.concatenate([scores[:, :edge], near], axis=1) if edge else near
        peak = jnp.max(scores, axis=-1, keepdims=True)
        exponent = jnp.exp2((scores - peak) * (dim ** (-0.5) * LOG2E))
        total = jnp.sum(exponent, axis=-1, keepdims=True)
        stacked = values[h, first : n + 1].reshape((n + 1 - first) * rows, dim)
        result = (mm(exponent.astype(jnp.bfloat16), stacked) / total).astype(jnp.bfloat16)
        out[at[n - 1], h, rows:] = result[:rows]
        out[at[n], h, rows:] = result[rows:]

    @pl.when(kind == 2)
    def _():
        state = [None for _ in heads]
        for n in range(pieces):
            for h in heads:
                state[h] = recur(h, n, state[h], None)
            if n % 2:
                for h in heads:
                    attend_pair(h, 0, n, wide)

    @pl.when(kind != 2)
    def _():
        keep = (kind == 1).astype(jnp.float32)
        reach = jnp.where(kind == 1, 2 * rows, rows)
        narrow = wide & ((row < rows) | (col >= 2 * rows - reach))
        for n in range(0, pieces, 2):
            for h in heads:
                recur(h, n + 1, recur(h, n, None, None), keep)
                attend_pair(h, n, n + 1, narrow)


def mix(meta, got, norm_gain):
    pieces, per, tall, dim = got.shape
    rows = (tall - GATE_ROWS) // 5
    together = 2 - per % 2
    gain = norm_gain.reshape(pieces, per, dim).transpose(1, 0, 2)
    return pl.pallas_call(
        mix_body,
        grid=(per // together,),
        in_specs=[
            pl.BlockSpec(memory_space=pltpu.SMEM),
            pl.BlockSpec((pieces, together, tall, dim), lambda h: (0, h, 0, 0)),
            pl.BlockSpec((together, pieces, dim), lambda h: (h, 0, 0)),
        ],
        out_specs=pl.BlockSpec((pieces, together, 2 * rows, dim), lambda h: (0, h, 0, 0)),
        out_shape=jax.ShapeDtypeStruct((pieces, per, 2 * rows, dim), jnp.bfloat16),
        scratch_shapes=[pltpu.VMEM((together, pieces, rows, dim), jnp.bfloat16)],
        compiler_params=pltpu.CompilerParams(vmem_limit_bytes=ROOM),
        name="mix",
    )(meta, got, gain)


def unpack_body(got, first, second):
    pieces, per, tall, dim = got.shape
    for head in range(pieces * per):
        columns = slice(head * dim, (head + 1) * dim)
        first[:, columns] = got[head // per, head % per, : tall // 2]
        second[:, columns] = got[head // per, head % per, tall // 2 :]


def unpack(got):
    pieces, per, tall, dim = got.shape
    whole = pl.BlockSpec(memory_space=pltpu.VMEM)
    shape = jax.ShapeDtypeStruct((tall // 2, pieces * per * dim), jnp.bfloat16)
    return pl.pallas_call(
        unpack_body,
        in_specs=[whole],
        out_specs=[whole, whole],
        out_shape=[shape, shape],
        compiler_params=pltpu.CompilerParams(vmem_limit_bytes=ROOM),
        name="unpack",
    )(got)


def document_body(gla_query, gla_key, gla_value, log_gates, norm_gain, attn_query, attn_key, doc_blocks):
    devices = lax.axis_size("ctx")
    pieces = devices // 2
    meta = find_place(doc_blocks)
    held = (gla_query, gla_key, gla_value, attn_query, attn_key, log_gates.T)
    members = []
    for start in range(devices - pieces + 1):
        inside = list(range(start, start + pieces))
        members.append([inside, [i for i in range(devices) if i not in inside]])
    for start in range(2):
        members.append([[(i + start) % devices, (i + start + 1) % devices] for i in range(0, devices, 2)])

    def exchange(x, groups):
        return lax.all_to_all(x, "ctx", split_axis=0, concat_axis=0, tiled=True, axis_index_groups=groups)

    def outward(groups):
        return lambda *held: exchange(pack(*held), groups)

    def homeward(groups):
        return lambda x: exchange(x, groups)

    got = lax.switch(meta[0], [outward(groups) for groups in members] + [pack], *held)
    mixed = mix(meta, got, norm_gain)
    back = lax.switch(meta[0], [homeward(groups) for groups in members] + [lambda x: x], mixed)
    return tuple(unpack(back))


def solution(mesh):
    placed = (
        P(("grp", "ctx"), None),
        P(("grp", "ctx"), None),
        P(("grp", "ctx"), None),
        P(("grp", "ctx"), None),
        P(),
        P(("grp", "ctx"), None),
        P(("grp", "ctx"), None),
        P("grp"),
    )
    parts, devices = mesh.shape["grp"], mesh.shape["ctx"]

    def step(gla_query, gla_key, gla_value, log_gates, norm_gain, attn_query, attn_key, doc_blocks):
        blocks = gla_query.shape[0] // parts // BLOCK
        documents = doc_blocks.shape[0] // parts
        longest = blocks // 2
        spare = blocks - longest - (documents - 1)
        heads = log_gates.shape[1]
        simple = blocks == devices and spare == 1 and heads % longest == 0 and longest * BLOCK <= WINDOW
        simple = simple and longest > 2 and longest % 2 == 0
        return jax.shard_map(
            document_body if simple else body,
            mesh=mesh,
            in_specs=placed,
            out_specs=(P(("grp", "ctx"), None), P(("grp", "ctx"), None)),
            check_vma=False,
        )(gla_query, gla_key, gla_value, log_gates, norm_gain, attn_query, attn_key, doc_blocks)

    return step
```

```python
import functools

import jax
import jax.numpy as jnp
from jax import lax
from jax.experimental import pallas as pl
from jax.experimental.pallas import tpu as pltpu
from jax.sharding import PartitionSpec as P

BLOCK = 128
WINDOW = 2048
GATE_ROWS = 8
LOG2E = 1.4426950408889634
ROOM = 24 * 2**20


def entering_2(part, axis, combine, identity):
    place = lax.axis_index(axis)
    gathered = jax.tree.map(lambda a: lax.all_gather(a, axis), part)
    state = jax.tree.map(lambda a, e: jnp.zeros_like(a) + jnp.asarray(e, a.dtype), part, identity)

    def one(turn, state):
        return combine(
            state, jax.tree.map(lambda a: lax.dynamic_index_in_dim(a, turn, 0, False), gathered)
        )

    return lax.fori_loop(0, place, one, state)


def compose(earlier, later):
    return (earlier[0] * later[0], later[0][:, None, None] * earlier[1] + later[1])


def gla_layer(gla_query, gla_key, gla_value, log_gates, norm_gain, doc_blocks):
    tok_rows, columns = gla_query.shape
    head_count = log_gates.shape[1]
    head_dim = columns // head_count
    block_count = tok_rows // BLOCK
    offset = lax.axis_index("ctx") * tok_rows
    doc_ends = jnp.cumsum(doc_blocks) * BLOCK
    starts = doc_ends - doc_blocks * BLOCK
    block_offsets = offset + jnp.arange(block_count, dtype=jnp.int32) * BLOCK
    resets = jnp.any(block_offsets[:, None] == starts[None, :], axis=1).astype(jnp.float32)
    shaped = (block_count, BLOCK, head_count, head_dim)
    query_rows = gla_query.reshape(shaped)
    key_rows = gla_key.reshape(shaped)
    float_query = query_rows.astype(jnp.float32) * head_dim ** (-0.5)
    float_key = key_rows.astype(jnp.float32)
    float_value = gla_value.reshape(shaped).astype(jnp.float32)
    gate_sums = jnp.cumsum(log_gates.reshape(block_count, BLOCK, head_count), axis=1)
    block_last = gate_sums[:, -1, :]
    by_head = gate_sums.transpose(0, 2, 1)
    causal = (jnp.arange(BLOCK)[:, None] >= jnp.arange(BLOCK)[None, :])[None, None]
    gaps = by_head[:, :, :, None] - by_head[:, :, None, :]
    weight = jnp.where(causal, jnp.exp(jnp.where(causal, gaps, 0.0)), 0.0)
    raw_scores = jnp.einsum(
        "cthd,cshd->chts", query_rows, key_rows, preferred_element_type=jnp.float32
    )
    scores = raw_scores * head_dim ** (-0.5) * weight
    inner_part = jnp.einsum("chts,cshd->cthd", scores, float_value, precision=lax.Precision.HIGHEST)
    tails = jnp.exp(block_last[:, None, :] - gate_sums)
    local_state = jnp.einsum(
        "cshd,cshe->chde",
        float_key * tails[..., None],
        float_value,
        precision=lax.Precision.HIGHEST,
    )
    decays = jnp.exp(block_last) * (1.0 - resets)[:, None]
    total_decay = jnp.ones((head_count,), jnp.float32)
    total_state = jnp.zeros((head_count, head_dim, head_dim), jnp.float32)
    block_id = 0
    total_decay, total_state = compose(
        (total_decay, total_state), (decays[block_id], local_state[block_id])
    )
    identity = (
        jnp.ones((head_count,), jnp.float32),
        jnp.zeros((head_count, head_dim, head_dim), jnp.float32),
    )
    incoming = entering_2((total_decay, total_state), "ctx", compose, identity)
    carried = incoming[1]
    block_id = 0
    entering = carried * (1.0 - resets[block_id])
    scaled_query = float_query[block_id] * jnp.exp(gate_sums[block_id])[..., None]
    outer_parts = [
        jnp.einsum("thd,hde->the", scaled_query, entering, precision=lax.Precision.HIGHEST)
    ]
    mixture = inner_part + jnp.stack(outer_parts)
    mean_square = jnp.mean(mixture * mixture, axis=-1, keepdims=True)
    rescaled_hidden = (
        mixture * lax.rsqrt(mean_square + 1e-06) * norm_gain.reshape(head_count, head_dim)
    )
    return rescaled_hidden.reshape(tok_rows, columns).astype(jnp.bfloat16)


def attend(my_queries, query_places, key_rows, value_rows, doc_ids, span_factor):
    all_rows, unit_heads, head_dim = key_rows.shape
    length = my_queries.shape[0]
    tile = min(512, length)
    span = tile * span_factor
    pad_key = jnp.concatenate(
        [
            jnp.zeros((WINDOW, unit_heads, head_dim), jnp.bfloat16),
            key_rows,
            jnp.zeros((span, unit_heads, head_dim), jnp.bfloat16),
        ]
    )
    pad_value = jnp.concatenate(
        [
            jnp.zeros((WINDOW, unit_heads, head_dim), jnp.bfloat16),
            value_rows,
            jnp.zeros((span, unit_heads, head_dim), jnp.bfloat16),
        ]
    )
    pad_docs = jnp.concatenate(
        [jnp.full((WINDOW,), -1, dtype=jnp.int32), doc_ids, jnp.full((span,), -1, dtype=jnp.int32)]
    )

    def one_tile(tile_index):
        tile_rows = lax.dynamic_slice_in_dim(my_queries, tile_index * tile, tile, 0)
        query_pos = lax.dynamic_slice_in_dim(query_places, tile_index * tile, tile, 0)
        first_pos = query_pos[0]
        key_block = lax.dynamic_slice_in_dim(pad_key, first_pos, WINDOW + span, 0)
        value_block = lax.dynamic_slice_in_dim(pad_value, first_pos, WINDOW + span, 0)
        key_docs = lax.dynamic_slice_in_dim(pad_docs, first_pos, WINDOW + span, 0)
        asker_documents = jnp.take(doc_ids, query_pos)
        key_pos = first_pos - WINDOW + jnp.arange(WINDOW + span, dtype=jnp.int32)
        allowed = (
            (key_pos[None, :] <= query_pos[:, None])
            & (key_pos[None, :] > query_pos[:, None] - WINDOW)
            & (key_docs[None, :] == asker_documents[:, None])
        )
        scores = jnp.einsum(
            "qhd,khd->hqk", tile_rows, key_block, preferred_element_type=jnp.float32
        ) * head_dim ** (-0.5)
        scores = jnp.where(allowed[None], scores, -1e30)
        row_peak = jnp.max(scores, axis=-1, keepdims=True)
        exponent = jnp.exp(scores - row_peak)
        weights = (exponent / jnp.sum(exponent, axis=-1, keepdims=True)).astype(jnp.bfloat16)
        return jnp.einsum(
            "hqk,khd->qhd", weights, value_block, preferred_element_type=jnp.float32
        ).astype(jnp.bfloat16)

    tiles_out = lax.map(one_tile, jnp.arange(length // tile, dtype=jnp.int32))
    return tiles_out.reshape(length, unit_heads, head_dim)


def body(gla_query, gla_key, gla_value, log_gates, norm_gain, attn_query, attn_key, doc_blocks):
    tok_rows, columns = attn_query.shape
    head_count = log_gates.shape[1]
    head_dim = columns // head_count
    devices = lax.axis_size("ctx")
    copies = max(1, devices // head_count)
    per_unit = max(1, head_count // devices)
    groups = head_count // per_unit
    share_rows = tok_rows // copies

    def to_heads(rows_in):
        spread_rows = rows_in.reshape(tok_rows, head_count, 1, head_dim)
        spread_rows = jnp.broadcast_to(spread_rows, (tok_rows, head_count, copies, head_dim))
        return spread_rows.reshape(tok_rows, devices, per_unit * head_dim)

    shared = attn_query.reshape(copies, share_rows, groups, per_unit * head_dim).transpose(
        1, 2, 0, 3
    )
    sent_query = shared.reshape(share_rows, devices, per_unit * head_dim)
    gla_mixed = gla_layer(gla_query, gla_key, gla_value, log_gates, norm_gain, doc_blocks)
    moved_query, moved_key, moved_value = (
        lax.all_to_all(sent_query, "ctx", split_axis=1, concat_axis=0, tiled=True),
        lax.all_to_all(to_heads(attn_key), "ctx", split_axis=1, concat_axis=0, tiled=True),
        lax.all_to_all(to_heads(gla_mixed), "ctx", split_axis=1, concat_axis=0, tiled=True),
    )
    all_rows = devices * tok_rows
    unit_shape = (all_rows, per_unit, head_dim)
    moved_query = moved_query.reshape(-1, per_unit, head_dim)
    moved_key = moved_key.reshape(unit_shape)
    moved_value = moved_value.reshape(unit_shape)
    doc_ends = jnp.cumsum(doc_blocks) * BLOCK
    positions = jnp.arange(all_rows, dtype=jnp.int32)
    doc_ids = jnp.sum((positions[:, None] >= doc_ends[None, :]).astype(jnp.int32), axis=1)
    local_replica = lax.axis_index("ctx") % copies
    query_places = (
        jnp.arange(devices, dtype=jnp.int32)[:, None] * tok_rows
        + local_replica * share_rows
        + jnp.arange(share_rows, dtype=jnp.int32)[None, :]
    ).reshape(-1)
    result = attend(moved_query, query_places, moved_key, moved_value, doc_ids, copies)
    outgoing = result.reshape(devices, share_rows, 1, per_unit * head_dim)
    returned = lax.all_to_all(outgoing, "ctx", split_axis=0, concat_axis=2, tiled=True)
    regrouped = returned.reshape(share_rows, groups, copies, per_unit, head_dim).transpose(
        2, 0, 1, 3, 4
    )
    attended = regrouped.reshape(tok_rows, head_count, head_dim)
    return (gla_mixed, attended.reshape(tok_rows, columns))


def scalar_layout(docs, place, pieces):
    end, kind, index, start = jnp.int32(0), jnp.int32(0), jnp.int32(0), jnp.int32(0)
    for d in range(docs.shape[0]):
        length = docs[d]
        inside = (place >= end) & (place < end + length)
        found = jnp.where(length == pieces, 2, jnp.where(length == 2, 1, 0))
        kind = jnp.where(inside, found, kind)
        index = jnp.where(inside, place - end, index)
        start = jnp.where(inside, end, start)
        end = end + length
    return kind, index, start


def place_body(docs, meta):
    pieces = lax.axis_size("ctx") // 2
    kind, index, start = scalar_layout(docs, lax.axis_index("ctx"), pieces)
    alone = lax.axis_size("ctx") - pieces + 3
    meta[0] = jnp.where(kind == 2, start, jnp.where(kind == 1, alone - 2 + start % 2, alone))
    meta[1] = kind
    meta[2] = index
    meta[3] = start


def find_place(docs):
    small = pl.BlockSpec(memory_space=pltpu.SMEM)
    return pl.pallas_call(
        place_body,
        in_specs=[small],
        out_specs=small,
        out_shape=jax.ShapeDtypeStruct((4,), jnp.int32),
        name="place",
    )(docs)


def pack_body(gq, gk, gv, aq, ak, gates, out):
    pieces, per, _, dim = out.shape
    rows = gq.shape[0]
    below = lax.broadcasted_iota(jnp.int32, (rows, rows), 0)
    until = lax.broadcasted_iota(jnp.int32, (rows, rows), 1)
    sums = jnp.dot(
        gates[...],
        (below <= until).astype(jnp.float32),
        precision=lax.Precision.HIGHEST,
        preferred_element_type=jnp.float32,
    )
    part = lax.broadcasted_iota(jnp.int32, (GATE_ROWS, rows), 0)
    for head in range(pieces * per):
        line = sums[head : head + 1, :] * LOG2E
        first = line.astype(jnp.bfloat16).astype(jnp.float32)
        rest = line - first
        second = rest.astype(jnp.bfloat16).astype(jnp.float32)
        third = rest - second
        tile = jnp.where(part == 0, first, jnp.where(part == 1, second, jnp.where(part == 2, third, 0.0)))
        out[head // per, head % per, 5 * rows :] = tile.astype(jnp.bfloat16)

    def piece(j, carry):
        for i, source in enumerate((gq, gk, gv, aq, ak)):
            for h in range(per):
                columns = pl.ds(pl.multiple_of((j * per + h) * dim, dim), dim)
                out[j, h, i * rows : (i + 1) * rows] = source[:, columns]
        return carry

    lax.fori_loop(0, pieces, piece, 0)


def pack(gq, gk, gv, aq, ak, gates):
    rows, columns = gq.shape
    heads = gates.shape[0]
    pieces = lax.axis_size("ctx") // 2
    whole = pl.BlockSpec(memory_space=pltpu.VMEM)
    return pl.pallas_call(
        pack_body,
        in_specs=[whole] * 6,
        out_specs=whole,
        out_shape=jax.ShapeDtypeStruct(
            (pieces, heads // pieces, 5 * rows + GATE_ROWS, columns // heads), jnp.bfloat16
        ),
        compiler_params=pltpu.CompilerParams(vmem_limit_bytes=ROOM),
        name="pack",
    )(gq, gk, gv, aq, ak, gates)


def mm(a, b):
    return jnp.dot(a, b, preferred_element_type=jnp.float32)


def mm_t(a, b):
    return lax.dot_general(a, b, (((1,), (1,)), ((), ())), preferred_element_type=jnp.float32)


def mix_body(meta, source, gain, out, got, values, arrived):
    pieces, _, _, dim = got.shape
    rows = values.shape[2]
    copies = [pltpu.make_async_copy(source.at[n], got.at[n], arrived.at[n]) for n in range(pieces)]
    for copy in copies:
        copy.start()
    kind, index = meta[1], meta[2]
    half = pieces // 2
    at, group = [], []
    for n in range(pieces):
        slot = jnp.where(kind == 1, (n % 2) * half + n // 2, n)
        at.append(slot)
        group.append(jnp.where(kind == 2, index, jnp.where(kind == 1, half * index + n // 2, n)))

    heads = range(got.shape[1])
    values[:, :, :, dim:] = jnp.ones(values.shape[:3] + (dim,), jnp.bfloat16)

    def part(at, h, n, i):
        return got[at[n], h, i * rows : (i + 1) * rows]

    row = lax.broadcasted_iota(jnp.int32, (2 * rows, 2 * rows), 0)
    col = lax.broadcasted_iota(jnp.int32, (2 * rows, 2 * rows), 1)
    wide = row >= col
    causal = wide[:rows, :rows]

    def recur(at, group, h, n, states, keep):
        state = states[h]
        query, key, value = part(at, h, n, 0), part(at, h, n, 1), part(at, h, n, 2)
        line = jnp.sum(got[at[n], h, 5 * rows :].astype(jnp.float32), axis=0, keepdims=True)
        across = jnp.broadcast_to(line, (rows, rows))
        products = mm_t(query, key)
        yield
        down = across.T
        turned = key.astype(jnp.float32).T
        yield
        last = down[rows - 1 : rows, :]
        tail = (turned * jnp.exp2(last - line)).astype(jnp.bfloat16)
        added = mm(tail, value)
        yield
        weight = jnp.where(causal, jnp.exp2(down - across), 0.0)
        inside = (products * weight).astype(jnp.bfloat16)
        yield
        if state is None:
            mixture = mm(inside, value)
            states[h] = added
        else:
            if keep is not None:
                state = state * keep
            far = (query.astype(jnp.float32) * jnp.exp2(down)).astype(jnp.bfloat16)
            mixture = mm(
                jnp.concatenate([inside, far], axis=1),
                jnp.concatenate([value, state.astype(jnp.bfloat16)], axis=0),
            )
            states[h] = state * jnp.exp2(last) + added
        yield
        square = jnp.mean(mixture * mixture, axis=-1, keepdims=True)
        yield
        mixed = mixture * lax.rsqrt(square + 1e-06 * dim) * gain[h, pl.ds(group[n], 1), :]
        mixed = mixed.astype(jnp.bfloat16)
        values[h, n, :, :dim] = mixed
        out[at[n], h, :rows] = mixed

    def attend_pair(at, h, first, n, open_):
        queries = jnp.concatenate([part(at, h, n - 1, 3), part(at, h, n, 3)], axis=0)
        keys = jnp.concatenate([part(at, h, m, 4) for m in range(first, n + 1)], axis=0)
        scores = mm_t(queries, keys)
        edge = (n - 1 - first) * rows
        near = jnp.where(open_, scores[:, edge:], -1e30)
        yield
        top = jnp.maximum(near[:, :rows], near[:, rows:])
        for m in range(edge // rows):
            top = jnp.maximum(top, scores[:, m * rows : (m + 1) * rows])
        yield
        peak = jnp.max(top, axis=-1, keepdims=True)
        yield
        parts = [near[:, :rows], near[:, rows:]]
        parts = [scores[:, m * rows : (m + 1) * rows] for m in range(edge // rows)] + parts
        exponents = []
        for s in parts:
            exponents.append(jnp.exp2((s - peak) * (dim ** (-0.5) * LOG2E)).astype(jnp.bfloat16))
            if len(exponents) % 2 == 0:
                yield
        stacked = values[h, first : n + 1].reshape((n + 1 - first) * rows, 2 * dim)
        both = mm(jnp.concatenate(exponents, axis=1), stacked)
        yield
        result = (both[:, :dim] / both[:, dim:]).astype(jnp.bfloat16)
        out[at[n - 1], h, rows:] = result[:rows]
        out[at[n], h, rows:] = result[rows:]

    def together(runs):
        while runs:
            runs = [run for run in runs if next(run, True) is None]

    def in_one():
        states = [None for _ in heads]
        straight = list(range(pieces))
        whole = [index] * pieces
        waiting = []
        for n in range(pieces):
            copies[n].wait()
            late = waiting if n % 2 == 0 else []
            together([recur(straight, whole, h, n, states, None) for h in heads] + late)
            if n % 2:
                waiting = [attend_pair(straight, h, 0, n, wide) for h in heads]
        together(waiting)

    def in_twos():
        for copy in copies:
            copy.wait()
        keep = (kind == 1).astype(jnp.float32)
        reach = jnp.where(kind == 1, 2 * rows, rows)
        narrow = wide & ((row < rows) | (col >= 2 * rows - reach))
        for n in range(0, pieces, 2):
            states = [None for _ in heads]
            for m, link in ((n, None), (n + 1, keep)):
                together([recur(at, group, h, m, states, link) for h in heads])
            together([attend_pair(at, h, n, n + 1, narrow) for h in heads])

    lax.cond(kind == 2, in_one, in_twos)


def mix(meta, got, norm_gain):
    pieces, per, tall, dim = got.shape
    rows = (tall - GATE_ROWS) // 5
    gain = norm_gain.reshape(pieces, per, dim).transpose(1, 0, 2)
    whole = pl.BlockSpec(memory_space=pltpu.VMEM)
    return pl.pallas_call(
        mix_body,
        in_specs=[
            pl.BlockSpec(memory_space=pltpu.SMEM),
            pl.BlockSpec(memory_space=pl.ANY),
            whole,
        ],
        out_specs=whole,
        out_shape=jax.ShapeDtypeStruct((pieces, per, 2 * rows, dim), jnp.bfloat16),
        scratch_shapes=[
            pltpu.VMEM(got.shape, jnp.bfloat16),
            pltpu.VMEM((per, pieces, rows, 2 * dim), jnp.bfloat16),
            pltpu.SemaphoreType.DMA((pieces,)),
        ],
        compiler_params=pltpu.CompilerParams(vmem_limit_bytes=ROOM),
        name="mix",
    )(meta, got, gain)


def unpack_body(got, first, second):
    pieces, per, tall, dim = got.shape
    for head in range(pieces * per):
        columns = slice(head * dim, (head + 1) * dim)
        first[:, columns] = got[head // per, head % per, : tall // 2]
        second[:, columns] = got[head // per, head % per, tall // 2 :]


def unpack(got):
    pieces, per, tall, dim = got.shape
    whole = pl.BlockSpec(memory_space=pltpu.VMEM)
    shape = jax.ShapeDtypeStruct((tall // 2, pieces * per * dim), jnp.bfloat16)
    return pl.pallas_call(
        unpack_body,
        in_specs=[whole],
        out_specs=[whole, whole],
        out_shape=[shape, shape],
        compiler_params=pltpu.CompilerParams(vmem_limit_bytes=ROOM),
        name="unpack",
    )(got)


def document_body(gla_query, gla_key, gla_value, log_gates, norm_gain, attn_query, attn_key, doc_blocks):
    devices = lax.axis_size("ctx")
    pieces = devices // 2
    meta = find_place(doc_blocks)
    held = (gla_query, gla_key, gla_value, attn_query, attn_key, log_gates.T)
    members = []
    for start in range(devices - pieces + 1):
        inside = list(range(start, start + pieces))
        members.append([inside, [i for i in range(devices) if i not in inside]])
    for start in range(2):
        members.append([[(i + start) % devices, (i + start + 1) % devices] for i in range(0, devices, 2)])

    def exchange(x, groups):
        return lax.all_to_all(x, "ctx", split_axis=0, concat_axis=0, tiled=True, axis_index_groups=groups)

    def outward(groups):
        return lambda *held: exchange(pack(*held), groups)

    def homeward(groups):
        return lambda x: exchange(x, groups)

    got = lax.switch(meta[0], [outward(groups) for groups in members] + [pack], *held)
    mixed = mix(meta, got, norm_gain)
    back = lax.switch(meta[0], [homeward(groups) for groups in members] + [lambda x: x], mixed)
    return tuple(unpack(back))


def solution(mesh):
    placed = (
        P(("grp", "ctx"), None),
        P(("grp", "ctx"), None),
        P(("grp", "ctx"), None),
        P(("grp", "ctx"), None),
        P(),
        P(("grp", "ctx"), None),
        P(("grp", "ctx"), None),
        P("grp"),
    )
    parts, devices = mesh.shape["grp"], mesh.shape["ctx"]

    def step(gla_query, gla_key, gla_value, log_gates, norm_gain, attn_query, attn_key, doc_blocks):
        blocks = gla_query.shape[0] // parts // BLOCK
        documents = doc_blocks.shape[0] // parts
        longest = blocks // 2
        spare = blocks - longest - (documents - 1)
        heads = log_gates.shape[1]
        simple = blocks == devices and spare == 1 and heads % longest == 0 and longest * BLOCK <= WINDOW
        simple = simple and longest > 2 and longest % 2 == 0
        return jax.shard_map(
            document_body if simple else body,
            mesh=mesh,
            in_specs=placed,
            out_specs=(P(("grp", "ctx"), None), P(("grp", "ctx"), None)),
            check_vma=False,
        )(gla_query, gla_key, gla_value, log_gates, norm_gain, attn_query, attn_key, doc_blocks)

    return step
```

```python
import functools

import jax
import jax.numpy as jnp
from jax import lax
from jax.experimental import pallas as pl
from jax.experimental.pallas import tpu as pltpu
from jax.sharding import PartitionSpec as P

BLOCK = 128
WINDOW = 2048
GATE_ROWS = 8
LOG2E = 1.4426950408889634
ROOM = 24 * 2**20


def entering_2(part, axis, combine, identity):
    place = lax.axis_index(axis)
    gathered = jax.tree.map(lambda a: lax.all_gather(a, axis), part)
    state = jax.tree.map(lambda a, e: jnp.zeros_like(a) + jnp.asarray(e, a.dtype), part, identity)

    def one(turn, state):
        return combine(
            state, jax.tree.map(lambda a: lax.dynamic_index_in_dim(a, turn, 0, False), gathered)
        )

    return lax.fori_loop(0, place, one, state)


def compose(earlier, later):
    return (earlier[0] * later[0], later[0][:, None, None] * earlier[1] + later[1])


def gla_layer(gla_query, gla_key, gla_value, log_gates, norm_gain, doc_blocks):
    tok_rows, columns = gla_query.shape
    head_count = log_gates.shape[1]
    head_dim = columns // head_count
    block_count = tok_rows // BLOCK
    offset = lax.axis_index("ctx") * tok_rows
    doc_ends = jnp.cumsum(doc_blocks) * BLOCK
    starts = doc_ends - doc_blocks * BLOCK
    block_offsets = offset + jnp.arange(block_count, dtype=jnp.int32) * BLOCK
    resets = jnp.any(block_offsets[:, None] == starts[None, :], axis=1).astype(jnp.float32)
    shaped = (block_count, BLOCK, head_count, head_dim)
    query_rows = gla_query.reshape(shaped)
    key_rows = gla_key.reshape(shaped)
    float_query = query_rows.astype(jnp.float32) * head_dim ** (-0.5)
    float_key = key_rows.astype(jnp.float32)
    float_value = gla_value.reshape(shaped).astype(jnp.float32)
    gate_sums = jnp.cumsum(log_gates.reshape(block_count, BLOCK, head_count), axis=1)
    block_last = gate_sums[:, -1, :]
    by_head = gate_sums.transpose(0, 2, 1)
    causal = (jnp.arange(BLOCK)[:, None] >= jnp.arange(BLOCK)[None, :])[None, None]
    gaps = by_head[:, :, :, None] - by_head[:, :, None, :]
    weight = jnp.where(causal, jnp.exp(jnp.where(causal, gaps, 0.0)), 0.0)
    raw_scores = jnp.einsum(
        "cthd,cshd->chts", query_rows, key_rows, preferred_element_type=jnp.float32
    )
    scores = raw_scores * head_dim ** (-0.5) * weight
    inner_part = jnp.einsum("chts,cshd->cthd", scores, float_value, precision=lax.Precision.HIGHEST)
    tails = jnp.exp(block_last[:, None, :] - gate_sums)
    local_state = jnp.einsum(
        "cshd,cshe->chde",
        float_key * tails[..., None],
        float_value,
        precision=lax.Precision.HIGHEST,
    )
    decays = jnp.exp(block_last) * (1.0 - resets)[:, None]
    total_decay = jnp.ones((head_count,), jnp.float32)
    total_state = jnp.zeros((head_count, head_dim, head_dim), jnp.float32)
    block_id = 0
    total_decay, total_state = compose(
        (total_decay, total_state), (decays[block_id], local_state[block_id])
    )
    identity = (
        jnp.ones((head_count,), jnp.float32),
        jnp.zeros((head_count, head_dim, head_dim), jnp.float32),
    )
    incoming = entering_2((total_decay, total_state), "ctx", compose, identity)
    carried = incoming[1]
    block_id = 0
    entering = carried * (1.0 - resets[block_id])
    scaled_query = float_query[block_id] * jnp.exp(gate_sums[block_id])[..., None]
    outer_parts = [
        jnp.einsum("thd,hde->the", scaled_query, entering, precision=lax.Precision.HIGHEST)
    ]
    mixture = inner_part + jnp.stack(outer_parts)
    mean_square = jnp.mean(mixture * mixture, axis=-1, keepdims=True)
    rescaled_hidden = (
        mixture * lax.rsqrt(mean_square + 1e-06) * norm_gain.reshape(head_count, head_dim)
    )
    return rescaled_hidden.reshape(tok_rows, columns).astype(jnp.bfloat16)


def attend(my_queries, query_places, key_rows, value_rows, doc_ids, span_factor):
    all_rows, unit_heads, head_dim = key_rows.shape
    length = my_queries.shape[0]
    tile = min(512, length)
    span = tile * span_factor
    pad_key = jnp.concatenate(
        [
            jnp.zeros((WINDOW, unit_heads, head_dim), jnp.bfloat16),
            key_rows,
            jnp.zeros((span, unit_heads, head_dim), jnp.bfloat16),
        ]
    )
    pad_value = jnp.concatenate(
        [
            jnp.zeros((WINDOW, unit_heads, head_dim), jnp.bfloat16),
            value_rows,
            jnp.zeros((span, unit_heads, head_dim), jnp.bfloat16),
        ]
    )
    pad_docs = jnp.concatenate(
        [jnp.full((WINDOW,), -1, dtype=jnp.int32), doc_ids, jnp.full((span,), -1, dtype=jnp.int32)]
    )

    def one_tile(tile_index):
        tile_rows = lax.dynamic_slice_in_dim(my_queries, tile_index * tile, tile, 0)
        query_pos = lax.dynamic_slice_in_dim(query_places, tile_index * tile, tile, 0)
        first_pos = query_pos[0]
        key_block = lax.dynamic_slice_in_dim(pad_key, first_pos, WINDOW + span, 0)
        value_block = lax.dynamic_slice_in_dim(pad_value, first_pos, WINDOW + span, 0)
        key_docs = lax.dynamic_slice_in_dim(pad_docs, first_pos, WINDOW + span, 0)
        asker_documents = jnp.take(doc_ids, query_pos)
        key_pos = first_pos - WINDOW + jnp.arange(WINDOW + span, dtype=jnp.int32)
        allowed = (
            (key_pos[None, :] <= query_pos[:, None])
            & (key_pos[None, :] > query_pos[:, None] - WINDOW)
            & (key_docs[None, :] == asker_documents[:, None])
        )
        scores = jnp.einsum(
            "qhd,khd->hqk", tile_rows, key_block, preferred_element_type=jnp.float32
        ) * head_dim ** (-0.5)
        scores = jnp.where(allowed[None], scores, -1e30)
        row_peak = jnp.max(scores, axis=-1, keepdims=True)
        exponent = jnp.exp(scores - row_peak)
        weights = (exponent / jnp.sum(exponent, axis=-1, keepdims=True)).astype(jnp.bfloat16)
        return jnp.einsum(
            "hqk,khd->qhd", weights, value_block, preferred_element_type=jnp.float32
        ).astype(jnp.bfloat16)

    tiles_out = lax.map(one_tile, jnp.arange(length // tile, dtype=jnp.int32))
    return tiles_out.reshape(length, unit_heads, head_dim)


def body(gla_query, gla_key, gla_value, log_gates, norm_gain, attn_query, attn_key, doc_blocks):
    tok_rows, columns = attn_query.shape
    head_count = log_gates.shape[1]
    head_dim = columns // head_count
    devices = lax.axis_size("ctx")
    copies = max(1, devices // head_count)
    per_unit = max(1, head_count // devices)
    groups = head_count // per_unit
    share_rows = tok_rows // copies

    def to_heads(rows_in):
        spread_rows = rows_in.reshape(tok_rows, head_count, 1, head_dim)
        spread_rows = jnp.broadcast_to(spread_rows, (tok_rows, head_count, copies, head_dim))
        return spread_rows.reshape(tok_rows, devices, per_unit * head_dim)

    shared = attn_query.reshape(copies, share_rows, groups, per_unit * head_dim).transpose(
        1, 2, 0, 3
    )
    sent_query = shared.reshape(share_rows, devices, per_unit * head_dim)
    gla_mixed = gla_layer(gla_query, gla_key, gla_value, log_gates, norm_gain, doc_blocks)
    moved_query, moved_key, moved_value = (
        lax.all_to_all(sent_query, "ctx", split_axis=1, concat_axis=0, tiled=True),
        lax.all_to_all(to_heads(attn_key), "ctx", split_axis=1, concat_axis=0, tiled=True),
        lax.all_to_all(to_heads(gla_mixed), "ctx", split_axis=1, concat_axis=0, tiled=True),
    )
    all_rows = devices * tok_rows
    unit_shape = (all_rows, per_unit, head_dim)
    moved_query = moved_query.reshape(-1, per_unit, head_dim)
    moved_key = moved_key.reshape(unit_shape)
    moved_value = moved_value.reshape(unit_shape)
    doc_ends = jnp.cumsum(doc_blocks) * BLOCK
    positions = jnp.arange(all_rows, dtype=jnp.int32)
    doc_ids = jnp.sum((positions[:, None] >= doc_ends[None, :]).astype(jnp.int32), axis=1)
    local_replica = lax.axis_index("ctx") % copies
    query_places = (
        jnp.arange(devices, dtype=jnp.int32)[:, None] * tok_rows
        + local_replica * share_rows
        + jnp.arange(share_rows, dtype=jnp.int32)[None, :]
    ).reshape(-1)
    result = attend(moved_query, query_places, moved_key, moved_value, doc_ids, copies)
    outgoing = result.reshape(devices, share_rows, 1, per_unit * head_dim)
    returned = lax.all_to_all(outgoing, "ctx", split_axis=0, concat_axis=2, tiled=True)
    regrouped = returned.reshape(share_rows, groups, copies, per_unit, head_dim).transpose(
        2, 0, 1, 3, 4
    )
    attended = regrouped.reshape(tok_rows, head_count, head_dim)
    return (gla_mixed, attended.reshape(tok_rows, columns))


def scalar_layout(docs, place, pieces):
    end, kind, index, start = jnp.int32(0), jnp.int32(0), jnp.int32(0), jnp.int32(0)
    for d in range(docs.shape[0]):
        length = docs[d]
        inside = (place >= end) & (place < end + length)
        found = jnp.where(length == pieces, 2, jnp.where(length == 2, 1, 0))
        kind = jnp.where(inside, found, kind)
        index = jnp.where(inside, place - end, index)
        start = jnp.where(inside, end, start)
        end = end + length
    return kind, index, start


def place_body(docs, meta):
    pieces = lax.axis_size("ctx") // 2
    kind, index, start = scalar_layout(docs, lax.axis_index("ctx"), pieces)
    alone = lax.axis_size("ctx") - pieces + 3
    meta[0] = jnp.where(kind == 2, start, jnp.where(kind == 1, alone - 2 + start % 2, alone))
    meta[1] = kind
    meta[2] = index
    meta[3] = start


def find_place(docs):
    small = pl.BlockSpec(memory_space=pltpu.SMEM)
    return pl.pallas_call(
        place_body,
        in_specs=[small],
        out_specs=small,
        out_shape=jax.ShapeDtypeStruct((4,), jnp.int32),
        name="place",
    )(docs)


def pack_body(gq, gk, gv, aq, ak, gates, out, loaded, arrived):
    pieces, per, _, dim = out.shape
    rows = gq.shape[0]
    copies = [
        pltpu.make_async_copy(source, loaded.at[i], arrived.at[i])
        for i, source in enumerate((gq, gk, gv, aq, ak))
    ]
    for copy in copies:
        copy.start()
    below = lax.broadcasted_iota(jnp.int32, (rows, rows), 0)
    until = lax.broadcasted_iota(jnp.int32, (rows, rows), 1)
    sums = jnp.dot(
        gates[...],
        (below <= until).astype(jnp.float32),
        precision=lax.Precision.HIGHEST,
        preferred_element_type=jnp.float32,
    )
    part = lax.broadcasted_iota(jnp.int32, (GATE_ROWS, rows), 0)
    for head in range(pieces * per):
        line = sums[head : head + 1, :] * LOG2E
        first = line.astype(jnp.bfloat16).astype(jnp.float32)
        rest = line - first
        second = rest.astype(jnp.bfloat16).astype(jnp.float32)
        third = rest - second
        tile = jnp.where(part == 0, first, jnp.where(part == 1, second, jnp.where(part == 2, third, 0.0)))
        out[head // per, head % per, 5 * rows :] = tile.astype(jnp.bfloat16)

    for i, copy in enumerate(copies):
        copy.wait()

        def piece(j, carry):
            for h in range(per):
                columns = pl.ds(pl.multiple_of((j * per + h) * dim, dim), dim)
                out[j, h, i * rows : (i + 1) * rows] = loaded[i, :, columns]
            return carry

        lax.fori_loop(0, pieces, piece, 0)


def pack(gq, gk, gv, aq, ak, gates):
    rows, columns = gq.shape
    heads = gates.shape[0]
    pieces = lax.axis_size("ctx") // 2
    whole = pl.BlockSpec(memory_space=pltpu.VMEM)
    return pl.pallas_call(
        pack_body,
        in_specs=[pl.BlockSpec(memory_space=pltpu.HBM)] * 5 + [whole],
        out_specs=whole,
        out_shape=jax.ShapeDtypeStruct(
            (pieces, heads // pieces, 5 * rows + GATE_ROWS, columns // heads), jnp.bfloat16
        ),
        scratch_shapes=[pltpu.VMEM((5, rows, columns), jnp.bfloat16), pltpu.SemaphoreType.DMA((5,))],
        compiler_params=pltpu.CompilerParams(vmem_limit_bytes=ROOM),
        name="pack",
    )(gq, gk, gv, aq, ak, gates)


def mm(a, b):
    return jnp.dot(a, b, preferred_element_type=jnp.float32)


def mm_t(a, b):
    return lax.dot_general(a, b, (((1,), (1,)), ((), ())), preferred_element_type=jnp.float32)


def mix_body(meta, source, gain, out, got, values, arrived):
    pieces, _, _, dim = got.shape
    rows = values.shape[2]
    copies = [pltpu.make_async_copy(source.at[n], got.at[n], arrived.at[n]) for n in range(pieces)]
    for copy in copies:
        copy.start()
    kind, index = meta[1], meta[2]
    half = pieces // 2
    at, group = [], []
    for n in range(pieces):
        slot = jnp.where(kind == 1, (n % 2) * half + n // 2, n)
        at.append(slot)
        group.append(jnp.where(kind == 2, index, jnp.where(kind == 1, half * index + n // 2, n)))

    heads = range(got.shape[1])
    values[:, :, :, dim:] = jnp.ones(values.shape[:3] + (dim,), jnp.bfloat16)

    def part(at, h, n, i):
        return got[at[n], h, i * rows : (i + 1) * rows]

    row = lax.broadcasted_iota(jnp.int32, (2 * rows, 2 * rows), 0)
    col = lax.broadcasted_iota(jnp.int32, (2 * rows, 2 * rows), 1)
    wide = row >= col
    causal = wide[:rows, :rows]

    def recur(at, group, h, n, states, keep):
        state = states[h]
        query, key, value = part(at, h, n, 0), part(at, h, n, 1), part(at, h, n, 2)
        line = jnp.sum(got[at[n], h, 5 * rows :].astype(jnp.float32), axis=0, keepdims=True)
        across = jnp.broadcast_to(line, (rows, rows))
        products = mm_t(query, key)
        yield
        down = across.T
        turned = key.astype(jnp.float32).T
        yield
        last = down[rows - 1 : rows, :]
        tail = (turned * jnp.exp2(last - line)).astype(jnp.bfloat16)
        added = mm(tail, value)
        yield
        weight = jnp.where(causal, jnp.exp2(down - across), 0.0)
        inside = (products * weight).astype(jnp.bfloat16)
        yield
        if state is None:
            mixture = mm(inside, value)
            states[h] = added
        else:
            if keep is not None:
                state = state * keep
            far = (query.astype(jnp.float32) * jnp.exp2(down)).astype(jnp.bfloat16)
            mixture = mm(
                jnp.concatenate([inside, far], axis=1),
                jnp.concatenate([value, state.astype(jnp.bfloat16)], axis=0),
            )
            states[h] = state * jnp.exp2(last) + added
        yield
        square = jnp.mean(mixture * mixture, axis=-1, keepdims=True)
        yield
        mixed = mixture * lax.rsqrt(square + 1e-06 * dim) * gain[h, pl.ds(group[n], 1), :]
        mixed = mixed.astype(jnp.bfloat16)
        values[h, n, :, :dim] = mixed
        out[at[n], h, :rows] = mixed

    def attend_pair(at, h, first, n, open_):
        queries = jnp.concatenate([part(at, h, n - 1, 3), part(at, h, n, 3)], axis=0)
        keys = jnp.concatenate([part(at, h, m, 4) for m in range(first, n + 1)], axis=0)
        scores = mm_t(queries, keys)
        edge = (n - 1 - first) * rows
        near = jnp.where(open_, scores[:, edge:], -1e30)
        yield
        top = jnp.maximum(near[:, :rows], near[:, rows:])
        for m in range(edge // rows):
            top = jnp.maximum(top, scores[:, m * rows : (m + 1) * rows])
        yield
        peak = jnp.max(top, axis=-1, keepdims=True)
        yield
        parts = [near[:, :rows], near[:, rows:]]
        parts = [scores[:, m * rows : (m + 1) * rows] for m in range(edge // rows)] + parts
        exponents = []
        for s in parts:
            exponents.append(jnp.exp2((s - peak) * (dim ** (-0.5) * LOG2E)).astype(jnp.bfloat16))
            if len(exponents) % 2 == 0:
                yield
        stacked = values[h, first : n + 1].reshape((n + 1 - first) * rows, 2 * dim)
        both = mm(jnp.concatenate(exponents, axis=1), stacked)
        yield
        result = (both[:, :dim] / both[:, dim:]).astype(jnp.bfloat16)
        out[at[n - 1], h, rows:] = result[:rows]
        out[at[n], h, rows:] = result[rows:]

    def together(runs):
        while runs:
            runs = [run for run in runs if next(run, True) is None]

    def in_one():
        states = [None for _ in heads]
        straight = list(range(pieces))
        whole = [index] * pieces
        waiting = []
        for n in range(pieces):
            for copy in (copies[:2], copies[2:])[n // 2] if n in (0, 2) else ():
                copy.wait()
            late = waiting if n % 2 == 0 else []
            together([recur(straight, whole, h, n, states, None) for h in heads] + late)
            if n % 2:
                waiting = [attend_pair(straight, h, 0, n, wide) for h in heads]
        together(waiting)

    def in_twos():
        for copy in copies:
            copy.wait()
        keep = (kind == 1).astype(jnp.float32)
        reach = jnp.where(kind == 1, 2 * rows, rows)
        narrow = wide & ((row < rows) | (col >= 2 * rows - reach))
        for n in range(0, pieces, 2):
            states = [None for _ in heads]
            for m, link in ((n, None), (n + 1, keep)):
                together([recur(at, group, h, m, states, link) for h in heads])
            together([attend_pair(at, h, n, n + 1, narrow) for h in heads])

    lax.cond(kind == 2, in_one, in_twos)


def mix(meta, got, norm_gain):
    pieces, per, tall, dim = got.shape
    rows = (tall - GATE_ROWS) // 5
    gain = norm_gain.reshape(pieces, per, dim).transpose(1, 0, 2)
    whole = pl.BlockSpec(memory_space=pltpu.VMEM)
    return pl.pallas_call(
        mix_body,
        in_specs=[
            pl.BlockSpec(memory_space=pltpu.SMEM),
            pl.BlockSpec(memory_space=pl.ANY),
            whole,
        ],
        out_specs=whole,
        out_shape=jax.ShapeDtypeStruct((pieces, per, 2 * rows, dim), jnp.bfloat16),
        scratch_shapes=[
            pltpu.VMEM(got.shape, jnp.bfloat16),
            pltpu.VMEM((per, pieces, rows, 2 * dim), jnp.bfloat16),
            pltpu.SemaphoreType.DMA((pieces,)),
        ],
        compiler_params=pltpu.CompilerParams(vmem_limit_bytes=ROOM),
        name="mix",
    )(meta, got, gain)


def unpack_body(got, first, second, lined, sent):
    pieces, per, tall, dim = got.shape
    width = per * dim
    copies = []
    for j in range(pieces):
        columns = slice(j * width, (j + 1) * width)
        for i, target in enumerate((first, second)):
            for h in range(per):
                lined[i, j, :, h * dim : (h + 1) * dim] = got[j, h, i * tall // 2 : (i + 1) * tall // 2]
            copies.append(pltpu.make_async_copy(lined.at[i, j], target.at[:, columns], sent.at[i, j]))
            copies[-1].start()
    for copy in copies:
        copy.wait()


def unpack(got):
    pieces, per, tall, dim = got.shape
    shape = jax.ShapeDtypeStruct((tall // 2, pieces * per * dim), jnp.bfloat16)
    return pl.pallas_call(
        unpack_body,
        in_specs=[pl.BlockSpec(memory_space=pltpu.VMEM)],
        out_specs=[pl.BlockSpec(memory_space=pltpu.HBM)] * 2,
        out_shape=[shape, shape],
        scratch_shapes=[
            pltpu.VMEM((2, pieces, tall // 2, per * dim), jnp.bfloat16),
            pltpu.SemaphoreType.DMA((2, pieces)),
        ],
        compiler_params=pltpu.CompilerParams(vmem_limit_bytes=ROOM),
        name="unpack",
    )(got)


def document_body(gla_query, gla_key, gla_value, log_gates, norm_gain, attn_query, attn_key, doc_blocks):
    devices = lax.axis_size("ctx")
    pieces = devices // 2
    meta = find_place(doc_blocks)
    held = (gla_query, gla_key, gla_value, attn_query, attn_key, log_gates.T)
    members = []
    for start in range(devices - pieces + 1):
        inside = list(range(start, start + pieces))
        members.append([inside, [i for i in range(devices) if i not in inside]])
    for start in range(2):
        members.append([[(i + start) % devices, (i + start + 1) % devices] for i in range(0, devices, 2)])

    def exchange(x, groups):
        return lax.all_to_all(x, "ctx", split_axis=0, concat_axis=0, tiled=True, axis_index_groups=groups)

    def outward(groups):
        return lambda *held: exchange(pack(*held), groups)

    def homeward(groups):
        return lambda x: exchange(x, groups)

    got = lax.switch(meta[0], [outward(groups) for groups in members] + [pack], *held)
    mixed = mix(meta, got, norm_gain)
    back = lax.switch(meta[0], [homeward(groups) for groups in members] + [lambda x: x], mixed)
    return tuple(unpack(back))


def solution(mesh):
    placed = (
        P(("grp", "ctx"), None),
        P(("grp", "ctx"), None),
        P(("grp", "ctx"), None),
        P(("grp", "ctx"), None),
        P(),
        P(("grp", "ctx"), None),
        P(("grp", "ctx"), None),
        P("grp"),
    )
    parts, devices = mesh.shape["grp"], mesh.shape["ctx"]

    def step(gla_query, gla_key, gla_value, log_gates, norm_gain, attn_query, attn_key, doc_blocks):
        blocks = gla_query.shape[0] // parts // BLOCK
        documents = doc_blocks.shape[0] // parts
        longest = blocks // 2
        spare = blocks - longest - (documents - 1)
        heads = log_gates.shape[1]
        simple = blocks == devices and spare == 1 and heads % longest == 0 and longest * BLOCK <= WINDOW
        simple = simple and longest > 2 and longest % 2 == 0
        return jax.shard_map(
            document_body if simple else body,
            mesh=mesh,
            in_specs=placed,
            out_specs=(P(("grp", "ctx"), None), P(("grp", "ctx"), None)),
            check_vma=False,
        )(gla_query, gla_key, gla_value, log_gates, norm_gain, attn_query, attn_key, doc_blocks)

    return step
```

```python
import functools

import jax
import jax.numpy as jnp
from jax import lax
from jax.experimental import pallas as pl
from jax.experimental.pallas import tpu as pltpu
from jax.sharding import PartitionSpec as P

BLOCK = 128
WINDOW = 2048
GATE_ROWS = 8
LOG2E = 1.4426950408889634
ROOM = 24 * 2**20


def entering_2(part, axis, combine, identity):
    place = lax.axis_index(axis)
    gathered = jax.tree.map(lambda a: lax.all_gather(a, axis), part)
    state = jax.tree.map(lambda a, e: jnp.zeros_like(a) + jnp.asarray(e, a.dtype), part, identity)

    def one(turn, state):
        return combine(
            state, jax.tree.map(lambda a: lax.dynamic_index_in_dim(a, turn, 0, False), gathered)
        )

    return lax.fori_loop(0, place, one, state)


def compose(earlier, later):
    return (earlier[0] * later[0], later[0][:, None, None] * earlier[1] + later[1])


def gla_layer(gla_query, gla_key, gla_value, log_gates, norm_gain, doc_blocks):
    tok_rows, columns = gla_query.shape
    head_count = log_gates.shape[1]
    head_dim = columns // head_count
    block_count = tok_rows // BLOCK
    offset = lax.axis_index("ctx") * tok_rows
    doc_ends = jnp.cumsum(doc_blocks) * BLOCK
    starts = doc_ends - doc_blocks * BLOCK
    block_offsets = offset + jnp.arange(block_count, dtype=jnp.int32) * BLOCK
    resets = jnp.any(block_offsets[:, None] == starts[None, :], axis=1).astype(jnp.float32)
    shaped = (block_count, BLOCK, head_count, head_dim)
    query_rows = gla_query.reshape(shaped)
    key_rows = gla_key.reshape(shaped)
    float_query = query_rows.astype(jnp.float32) * head_dim ** (-0.5)
    float_key = key_rows.astype(jnp.float32)
    float_value = gla_value.reshape(shaped).astype(jnp.float32)
    gate_sums = jnp.cumsum(log_gates.reshape(block_count, BLOCK, head_count), axis=1)
    block_last = gate_sums[:, -1, :]
    by_head = gate_sums.transpose(0, 2, 1)
    causal = (jnp.arange(BLOCK)[:, None] >= jnp.arange(BLOCK)[None, :])[None, None]
    gaps = by_head[:, :, :, None] - by_head[:, :, None, :]
    weight = jnp.where(causal, jnp.exp(jnp.where(causal, gaps, 0.0)), 0.0)
    raw_scores = jnp.einsum(
        "cthd,cshd->chts", query_rows, key_rows, preferred_element_type=jnp.float32
    )
    scores = raw_scores * head_dim ** (-0.5) * weight
    inner_part = jnp.einsum("chts,cshd->cthd", scores, float_value, precision=lax.Precision.HIGHEST)
    tails = jnp.exp(block_last[:, None, :] - gate_sums)
    local_state = jnp.einsum(
        "cshd,cshe->chde",
        float_key * tails[..., None],
        float_value,
        precision=lax.Precision.HIGHEST,
    )
    decays = jnp.exp(block_last) * (1.0 - resets)[:, None]
    total_decay = jnp.ones((head_count,), jnp.float32)
    total_state = jnp.zeros((head_count, head_dim, head_dim), jnp.float32)
    block_id = 0
    total_decay, total_state = compose(
        (total_decay, total_state), (decays[block_id], local_state[block_id])
    )
    identity = (
        jnp.ones((head_count,), jnp.float32),
        jnp.zeros((head_count, head_dim, head_dim), jnp.float32),
    )
    incoming = entering_2((total_decay, total_state), "ctx", compose, identity)
    carried = incoming[1]
    block_id = 0
    entering = carried * (1.0 - resets[block_id])
    scaled_query = float_query[block_id] * jnp.exp(gate_sums[block_id])[..., None]
    outer_parts = [
        jnp.einsum("thd,hde->the", scaled_query, entering, precision=lax.Precision.HIGHEST)
    ]
    mixture = inner_part + jnp.stack(outer_parts)
    mean_square = jnp.mean(mixture * mixture, axis=-1, keepdims=True)
    rescaled_hidden = (
        mixture * lax.rsqrt(mean_square + 1e-06) * norm_gain.reshape(head_count, head_dim)
    )
    return rescaled_hidden.reshape(tok_rows, columns).astype(jnp.bfloat16)


def attend(my_queries, query_places, key_rows, value_rows, doc_ids, span_factor):
    all_rows, unit_heads, head_dim = key_rows.shape
    length = my_queries.shape[0]
    tile = min(512, length)
    span = tile * span_factor
    pad_key = jnp.concatenate(
        [
            jnp.zeros((WINDOW, unit_heads, head_dim), jnp.bfloat16),
            key_rows,
            jnp.zeros((span, unit_heads, head_dim), jnp.bfloat16),
        ]
    )
    pad_value = jnp.concatenate(
        [
            jnp.zeros((WINDOW, unit_heads, head_dim), jnp.bfloat16),
            value_rows,
            jnp.zeros((span, unit_heads, head_dim), jnp.bfloat16),
        ]
    )
    pad_docs = jnp.concatenate(
        [jnp.full((WINDOW,), -1, dtype=jnp.int32), doc_ids, jnp.full((span,), -1, dtype=jnp.int32)]
    )

    def one_tile(tile_index):
        tile_rows = lax.dynamic_slice_in_dim(my_queries, tile_index * tile, tile, 0)
        query_pos = lax.dynamic_slice_in_dim(query_places, tile_index * tile, tile, 0)
        first_pos = query_pos[0]
        key_block = lax.dynamic_slice_in_dim(pad_key, first_pos, WINDOW + span, 0)
        value_block = lax.dynamic_slice_in_dim(pad_value, first_pos, WINDOW + span, 0)
        key_docs = lax.dynamic_slice_in_dim(pad_docs, first_pos, WINDOW + span, 0)
        asker_documents = jnp.take(doc_ids, query_pos)
        key_pos = first_pos - WINDOW + jnp.arange(WINDOW + span, dtype=jnp.int32)
        allowed = (
            (key_pos[None, :] <= query_pos[:, None])
            & (key_pos[None, :] > query_pos[:, None] - WINDOW)
            & (key_docs[None, :] == asker_documents[:, None])
        )
        scores = jnp.einsum(
            "qhd,khd->hqk", tile_rows, key_block, preferred_element_type=jnp.float32
        ) * head_dim ** (-0.5)
        scores = jnp.where(allowed[None], scores, -1e30)
        row_peak = jnp.max(scores, axis=-1, keepdims=True)
        exponent = jnp.exp(scores - row_peak)
        weights = (exponent / jnp.sum(exponent, axis=-1, keepdims=True)).astype(jnp.bfloat16)
        return jnp.einsum(
            "hqk,khd->qhd", weights, value_block, preferred_element_type=jnp.float32
        ).astype(jnp.bfloat16)

    tiles_out = lax.map(one_tile, jnp.arange(length // tile, dtype=jnp.int32))
    return tiles_out.reshape(length, unit_heads, head_dim)


def body(gla_query, gla_key, gla_value, log_gates, norm_gain, attn_query, attn_key, doc_blocks):
    tok_rows, columns = attn_query.shape
    head_count = log_gates.shape[1]
    head_dim = columns // head_count
    devices = lax.axis_size("ctx")
    copies = max(1, devices // head_count)
    per_unit = max(1, head_count // devices)
    groups = head_count // per_unit
    share_rows = tok_rows // copies

    def to_heads(rows_in):
        spread_rows = rows_in.reshape(tok_rows, head_count, 1, head_dim)
        spread_rows = jnp.broadcast_to(spread_rows, (tok_rows, head_count, copies, head_dim))
        return spread_rows.reshape(tok_rows, devices, per_unit * head_dim)

    shared = attn_query.reshape(copies, share_rows, groups, per_unit * head_dim).transpose(
        1, 2, 0, 3
    )
    sent_query = shared.reshape(share_rows, devices, per_unit * head_dim)
    gla_mixed = gla_layer(gla_query, gla_key, gla_value, log_gates, norm_gain, doc_blocks)
    moved_query, moved_key, moved_value = (
        lax.all_to_all(sent_query, "ctx", split_axis=1, concat_axis=0, tiled=True),
        lax.all_to_all(to_heads(attn_key), "ctx", split_axis=1, concat_axis=0, tiled=True),
        lax.all_to_all(to_heads(gla_mixed), "ctx", split_axis=1, concat_axis=0, tiled=True),
    )
    all_rows = devices * tok_rows
    unit_shape = (all_rows, per_unit, head_dim)
    moved_query = moved_query.reshape(-1, per_unit, head_dim)
    moved_key = moved_key.reshape(unit_shape)
    moved_value = moved_value.reshape(unit_shape)
    doc_ends = jnp.cumsum(doc_blocks) * BLOCK
    positions = jnp.arange(all_rows, dtype=jnp.int32)
    doc_ids = jnp.sum((positions[:, None] >= doc_ends[None, :]).astype(jnp.int32), axis=1)
    local_replica = lax.axis_index("ctx") % copies
    query_places = (
        jnp.arange(devices, dtype=jnp.int32)[:, None] * tok_rows
        + local_replica * share_rows
        + jnp.arange(share_rows, dtype=jnp.int32)[None, :]
    ).reshape(-1)
    result = attend(moved_query, query_places, moved_key, moved_value, doc_ids, copies)
    outgoing = result.reshape(devices, share_rows, 1, per_unit * head_dim)
    returned = lax.all_to_all(outgoing, "ctx", split_axis=0, concat_axis=2, tiled=True)
    regrouped = returned.reshape(share_rows, groups, copies, per_unit, head_dim).transpose(
        2, 0, 1, 3, 4
    )
    attended = regrouped.reshape(tok_rows, head_count, head_dim)
    return (gla_mixed, attended.reshape(tok_rows, columns))


def scalar_layout(docs, place, pieces):
    end, kind, index, start = jnp.int32(0), jnp.int32(0), jnp.int32(0), jnp.int32(0)
    for d in range(docs.shape[0]):
        length = docs[d]
        inside = (place >= end) & (place < end + length)
        found = jnp.where(length == pieces, 2, jnp.where(length == 2, 1, 0))
        kind = jnp.where(inside, found, kind)
        index = jnp.where(inside, place - end, index)
        start = jnp.where(inside, end, start)
        end = end + length
    return kind, index, start


def place_body(docs, meta):
    pieces = lax.axis_size("ctx") // 2
    kind, index, start = scalar_layout(docs, lax.axis_index("ctx"), pieces)
    alone = lax.axis_size("ctx") - pieces + 3
    meta[0] = jnp.where(kind == 2, start, jnp.where(kind == 1, alone - 2 + start % 2, alone))
    meta[1] = kind
    meta[2] = index
    meta[3] = start


def find_place(docs):
    small = pl.BlockSpec(memory_space=pltpu.SMEM)
    return pl.pallas_call(
        place_body,
        in_specs=[small],
        out_specs=small,
        out_shape=jax.ShapeDtypeStruct((4,), jnp.int32),
        compiler_params=pltpu.CompilerParams(vmem_limit_bytes=ROOM),
        name="place",
    )(pltpu.with_memory_space_constraint(docs, pltpu.HBM))


def pack_body(gq, gk, gv, aq, ak, gates, out, loaded, arrived):
    pieces, per, _, dim = out.shape
    rows = gq.shape[0]
    copies = [
        pltpu.make_async_copy(source, loaded.at[i], arrived.at[i])
        for i, source in enumerate((gq, gk, gv, aq, ak))
    ]
    for copy in copies:
        copy.start()
    below = lax.broadcasted_iota(jnp.int32, (rows, rows), 0)
    until = lax.broadcasted_iota(jnp.int32, (rows, rows), 1)
    sums = jnp.dot(
        gates[...],
        (below <= until).astype(jnp.float32),
        precision=lax.Precision.HIGHEST,
        preferred_element_type=jnp.float32,
    )
    part = lax.broadcasted_iota(jnp.int32, (GATE_ROWS, rows), 0)
    for head in range(pieces * per):
        line = sums[head : head + 1, :] * LOG2E
        first = line.astype(jnp.bfloat16).astype(jnp.float32)
        rest = line - first
        second = rest.astype(jnp.bfloat16).astype(jnp.float32)
        third = rest - second
        tile = jnp.where(part == 0, first, jnp.where(part == 1, second, jnp.where(part == 2, third, 0.0)))
        out[head // per, head % per, 5 * rows :] = tile.astype(jnp.bfloat16)

    for i, copy in enumerate(copies):
        copy.wait()

        def piece(j, carry):
            for h in range(per):
                columns = pl.ds(pl.multiple_of((j * per + h) * dim, dim), dim)
                out[j, h, i * rows : (i + 1) * rows] = loaded[i, :, columns]
            return carry

        lax.fori_loop(0, pieces, piece, 0)


def pack(gq, gk, gv, aq, ak, gates):
    rows, columns = gq.shape
    heads = gates.shape[0]
    pieces = lax.axis_size("ctx") // 2
    whole = pl.BlockSpec(memory_space=pltpu.VMEM)
    return pl.pallas_call(
        pack_body,
        in_specs=[pl.BlockSpec(memory_space=pltpu.HBM)] * 5 + [whole],
        out_specs=whole,
        out_shape=jax.ShapeDtypeStruct(
            (pieces, heads // pieces, 5 * rows + GATE_ROWS, columns // heads), jnp.bfloat16
        ),
        scratch_shapes=[pltpu.VMEM((5, rows, columns), jnp.bfloat16), pltpu.SemaphoreType.DMA((5,))],
        compiler_params=pltpu.CompilerParams(vmem_limit_bytes=ROOM),
        name="pack",
    )(gq, gk, gv, aq, ak, gates)


def mm(a, b):
    return jnp.dot(a, b, preferred_element_type=jnp.float32)


def mm_t(a, b):
    return lax.dot_general(a, b, (((1,), (1,)), ((), ())), preferred_element_type=jnp.float32)


def mix_body(meta, source, gain, out, got, values, arrived):
    pieces, _, _, dim = got.shape
    rows = values.shape[2]
    copies = [pltpu.make_async_copy(source.at[n], got.at[n], arrived.at[n]) for n in range(pieces)]
    for copy in copies:
        copy.start()
    kind, index = meta[1], meta[2]
    half = pieces // 2
    at, group = [], []
    for n in range(pieces):
        slot = jnp.where(kind == 1, (n % 2) * half + n // 2, n)
        at.append(slot)
        group.append(jnp.where(kind == 2, index, jnp.where(kind == 1, half * index + n // 2, n)))

    heads = range(got.shape[1])
    values[:, :, :, dim:] = jnp.ones(values.shape[:3] + (dim,), jnp.bfloat16)

    def part(at, h, n, i):
        return got[at[n], h, i * rows : (i + 1) * rows]

    row = lax.broadcasted_iota(jnp.int32, (2 * rows, 2 * rows), 0)
    col = lax.broadcasted_iota(jnp.int32, (2 * rows, 2 * rows), 1)
    wide = row >= col
    causal = wide[:rows, :rows]

    def recur(at, group, h, n, states, keep):
        state = states[h]
        query, key, value = part(at, h, n, 0), part(at, h, n, 1), part(at, h, n, 2)
        line = jnp.sum(got[at[n], h, 5 * rows :].astype(jnp.float32), axis=0, keepdims=True)
        across = jnp.broadcast_to(line, (rows, rows))
        products = mm_t(query, key)
        yield
        down = across.T
        turned = key.astype(jnp.float32).T
        yield
        last = down[rows - 1 : rows, :]
        tail = (turned * jnp.exp2(last - line)).astype(jnp.bfloat16)
        added = mm(tail, value)
        yield
        weight = jnp.where(causal, jnp.exp2(down - across), 0.0)
        inside = (products * weight).astype(jnp.bfloat16)
        yield
        if state is None:
            mixture = mm(inside, value)
            states[h] = added
        else:
            if keep is not None:
                state = state * keep
            far = (query.astype(jnp.float32) * jnp.exp2(down)).astype(jnp.bfloat16)
            mixture = mm(
                jnp.concatenate([inside, far], axis=1),
                jnp.concatenate([value, state.astype(jnp.bfloat16)], axis=0),
            )
            states[h] = state * jnp.exp2(last) + added
        yield
        square = jnp.mean(mixture * mixture, axis=-1, keepdims=True)
        yield
        mixed = mixture * lax.rsqrt(square + 1e-06 * dim) * gain[h, pl.ds(group[n], 1), :]
        mixed = mixed.astype(jnp.bfloat16)
        values[h, n, :, :dim] = mixed
        out[at[n], h, :rows] = mixed

    def attend_pair(at, h, first, n, open_):
        queries = jnp.concatenate([part(at, h, n - 1, 3), part(at, h, n, 3)], axis=0)
        keys = jnp.concatenate([part(at, h, m, 4) for m in range(first, n + 1)], axis=0)
        scores = mm_t(queries, keys)
        edge = (n - 1 - first) * rows
        near = jnp.where(open_, scores[:, edge:], -1e30)
        yield
        top = jnp.maximum(near[:, :rows], near[:, rows:])
        for m in range(edge // rows):
            top = jnp.maximum(top, scores[:, m * rows : (m + 1) * rows])
        yield
        peak = jnp.max(top, axis=-1, keepdims=True)
        yield
        parts = [near[:, :rows], near[:, rows:]]
        parts = [scores[:, m * rows : (m + 1) * rows] for m in range(edge // rows)] + parts
        exponents = []
        for s in parts:
            exponents.append(jnp.exp2((s - peak) * (dim ** (-0.5) * LOG2E)).astype(jnp.bfloat16))
            if len(exponents) % 2 == 0:
                yield
        stacked = values[h, first : n + 1].reshape((n + 1 - first) * rows, 2 * dim)
        both = mm(jnp.concatenate(exponents, axis=1), stacked)
        yield
        result = (both[:, :dim] / both[:, dim:]).astype(jnp.bfloat16)
        out[at[n - 1], h, rows:] = result[:rows]
        out[at[n], h, rows:] = result[rows:]

    def together(runs):
        while runs:
            runs = [run for run in runs if next(run, True) is None]

    def in_one():
        states = [None for _ in heads]
        straight = list(range(pieces))
        whole = [index] * pieces
        waiting = []
        for n in range(pieces):
            for copy in (copies[:2], copies[2:4], copies[4:])[n // 2] if n in (0, 2, 4) else ():
                copy.wait()
            late = waiting if n % 2 == 0 else []
            together([recur(straight, whole, h, n, states, None) for h in heads] + late)
            if n % 2:
                waiting = [attend_pair(straight, h, 0, n, wide) for h in heads]
        together(waiting)

    def in_twos():
        for copy in copies:
            copy.wait()
        keep = (kind == 1).astype(jnp.float32)
        reach = jnp.where(kind == 1, 2 * rows, rows)
        narrow = wide & ((row < rows) | (col >= 2 * rows - reach))
        for n in range(0, pieces, 2):
            states = [None for _ in heads]
            for m, link in ((n, None), (n + 1, keep)):
                together([recur(at, group, h, m, states, link) for h in heads])
            together([attend_pair(at, h, n, n + 1, narrow) for h in heads])

    lax.cond(kind == 2, in_one, in_twos)


def mix(meta, got, norm_gain):
    pieces, per, tall, dim = got.shape
    rows = (tall - GATE_ROWS) // 5
    gain = norm_gain.reshape(pieces, per, dim).transpose(1, 0, 2)
    whole = pl.BlockSpec(memory_space=pltpu.VMEM)
    return pl.pallas_call(
        mix_body,
        in_specs=[
            pl.BlockSpec(memory_space=pltpu.SMEM),
            pl.BlockSpec(memory_space=pl.ANY),
            whole,
        ],
        out_specs=whole,
        out_shape=jax.ShapeDtypeStruct((pieces, per, 2 * rows, dim), jnp.bfloat16),
        scratch_shapes=[
            pltpu.VMEM(got.shape, jnp.bfloat16),
            pltpu.VMEM((per, pieces, rows, 2 * dim), jnp.bfloat16),
            pltpu.SemaphoreType.DMA((pieces,)),
        ],
        compiler_params=pltpu.CompilerParams(vmem_limit_bytes=ROOM),
        name="mix",
    )(meta, got, gain)


def unpack_body(got, first, second, lined, sent):
    pieces, per, tall, dim = got.shape
    width = per * dim
    copies = []
    for j in range(pieces):
        columns = slice(j * width, (j + 1) * width)
        for i, target in enumerate((first, second)):
            for h in range(per):
                lined[i, j, :, h * dim : (h + 1) * dim] = got[j, h, i * tall // 2 : (i + 1) * tall // 2]
            copies.append(pltpu.make_async_copy(lined.at[i, j], target.at[:, columns], sent.at[i, j]))
            copies[-1].start()
    for copy in copies:
        copy.wait()


def unpack(got):
    pieces, per, tall, dim = got.shape
    shape = jax.ShapeDtypeStruct((tall // 2, pieces * per * dim), jnp.bfloat16)
    return pl.pallas_call(
        unpack_body,
        in_specs=[pl.BlockSpec(memory_space=pltpu.VMEM)],
        out_specs=[pl.BlockSpec(memory_space=pltpu.HBM)] * 2,
        out_shape=[shape, shape],
        scratch_shapes=[
            pltpu.VMEM((2, pieces, tall // 2, per * dim), jnp.bfloat16),
            pltpu.SemaphoreType.DMA((2, pieces)),
        ],
        compiler_params=pltpu.CompilerParams(vmem_limit_bytes=ROOM),
        name="unpack",
    )(got)


def document_body(gla_query, gla_key, gla_value, log_gates, norm_gain, attn_query, attn_key, doc_blocks):
    devices = lax.axis_size("ctx")
    pieces = devices // 2
    meta = find_place(doc_blocks)
    held = (gla_query, gla_key, gla_value, attn_query, attn_key, log_gates.T)
    members = []
    for start in range(devices - pieces + 1):
        inside = list(range(start, start + pieces))
        members.append([inside, [i for i in range(devices) if i not in inside]])
    for start in range(2):
        members.append([[(i + start) % devices, (i + start + 1) % devices] for i in range(0, devices, 2)])

    def exchange(x, groups):
        return lax.all_to_all(x, "ctx", split_axis=0, concat_axis=0, tiled=True, axis_index_groups=groups)

    def outward(groups):
        return lambda *held: exchange(pack(*held), groups)

    def homeward(groups):
        return lambda x: exchange(x, groups)

    got = lax.switch(meta[0], [outward(groups) for groups in members] + [pack], *held)
    mixed = mix(meta, got, norm_gain)
    back = lax.switch(meta[0], [homeward(groups) for groups in members] + [lambda x: x], mixed)
    return tuple(unpack(back))


def solution(mesh):
    placed = (
        P(("grp", "ctx"), None),
        P(("grp", "ctx"), None),
        P(("grp", "ctx"), None),
        P(("grp", "ctx"), None),
        P(),
        P(("grp", "ctx"), None),
        P(("grp", "ctx"), None),
        P("grp"),
    )
    parts, devices = mesh.shape["grp"], mesh.shape["ctx"]

    def step(gla_query, gla_key, gla_value, log_gates, norm_gain, attn_query, attn_key, doc_blocks):
        blocks = gla_query.shape[0] // parts // BLOCK
        documents = doc_blocks.shape[0] // parts
        longest = blocks // 2
        spare = blocks - longest - (documents - 1)
        heads = log_gates.shape[1]
        simple = blocks == devices and spare == 1 and heads % longest == 0 and longest * BLOCK <= WINDOW
        simple = simple and longest > 2 and longest % 2 == 0
        return jax.shard_map(
            document_body if simple else body,
            mesh=mesh,
            in_specs=placed,
            out_specs=(P(("grp", "ctx"), None), P(("grp", "ctx"), None)),
            check_vma=False,
        )(gla_query, gla_key, gla_value, log_gates, norm_gain, attn_query, attn_key, doc_blocks)

    return step
```

```python
import functools

import jax
import jax.numpy as jnp
from jax import lax
from jax.experimental import pallas as pl
from jax.experimental.pallas import tpu as pltpu
from jax.sharding import PartitionSpec as P

BLOCK = 128
WINDOW = 2048
LOG2E = 1.4426950408889634
ROOM = 24 * 2**20


def entering_2(part, axis, combine, identity):
    place = lax.axis_index(axis)
    gathered = jax.tree.map(lambda a: lax.all_gather(a, axis), part)
    state = jax.tree.map(lambda a, e: jnp.zeros_like(a) + jnp.asarray(e, a.dtype), part, identity)

    def one(turn, state):
        return combine(
            state, jax.tree.map(lambda a: lax.dynamic_index_in_dim(a, turn, 0, False), gathered)
        )

    return lax.fori_loop(0, place, one, state)


def compose(earlier, later):
    return (earlier[0] * later[0], later[0][:, None, None] * earlier[1] + later[1])


def gla_layer(gla_query, gla_key, gla_value, log_gates, norm_gain, doc_blocks):
    tok_rows, columns = gla_query.shape
    head_count = log_gates.shape[1]
    head_dim = columns // head_count
    block_count = tok_rows // BLOCK
    offset = lax.axis_index("ctx") * tok_rows
    doc_ends = jnp.cumsum(doc_blocks) * BLOCK
    starts = doc_ends - doc_blocks * BLOCK
    block_offsets = offset + jnp.arange(block_count, dtype=jnp.int32) * BLOCK
    resets = jnp.any(block_offsets[:, None] == starts[None, :], axis=1).astype(jnp.float32)
    shaped = (block_count, BLOCK, head_count, head_dim)
    query_rows = gla_query.reshape(shaped)
    key_rows = gla_key.reshape(shaped)
    float_query = query_rows.astype(jnp.float32) * head_dim ** (-0.5)
    float_key = key_rows.astype(jnp.float32)
    float_value = gla_value.reshape(shaped).astype(jnp.float32)
    gate_sums = jnp.cumsum(log_gates.reshape(block_count, BLOCK, head_count), axis=1)
    block_last = gate_sums[:, -1, :]
    by_head = gate_sums.transpose(0, 2, 1)
    causal = (jnp.arange(BLOCK)[:, None] >= jnp.arange(BLOCK)[None, :])[None, None]
    gaps = by_head[:, :, :, None] - by_head[:, :, None, :]
    weight = jnp.where(causal, jnp.exp(jnp.where(causal, gaps, 0.0)), 0.0)
    raw_scores = jnp.einsum(
        "cthd,cshd->chts", query_rows, key_rows, preferred_element_type=jnp.float32
    )
    scores = raw_scores * head_dim ** (-0.5) * weight
    inner_part = jnp.einsum("chts,cshd->cthd", scores, float_value, precision=lax.Precision.HIGHEST)
    tails = jnp.exp(block_last[:, None, :] - gate_sums)
    local_state = jnp.einsum(
        "cshd,cshe->chde",
        float_key * tails[..., None],
        float_value,
        precision=lax.Precision.HIGHEST,
    )
    decays = jnp.exp(block_last) * (1.0 - resets)[:, None]
    total_decay = jnp.ones((head_count,), jnp.float32)
    total_state = jnp.zeros((head_count, head_dim, head_dim), jnp.float32)
    block_id = 0
    total_decay, total_state = compose(
        (total_decay, total_state), (decays[block_id], local_state[block_id])
    )
    identity = (
        jnp.ones((head_count,), jnp.float32),
        jnp.zeros((head_count, head_dim, head_dim), jnp.float32),
    )
    incoming = entering_2((total_decay, total_state), "ctx", compose, identity)
    carried = incoming[1]
    block_id = 0
    entering = carried * (1.0 - resets[block_id])
    scaled_query = float_query[block_id] * jnp.exp(gate_sums[block_id])[..., None]
    outer_parts = [
        jnp.einsum("thd,hde->the", scaled_query, entering, precision=lax.Precision.HIGHEST)
    ]
    mixture = inner_part + jnp.stack(outer_parts)
    mean_square = jnp.mean(mixture * mixture, axis=-1, keepdims=True)
    rescaled_hidden = (
        mixture * lax.rsqrt(mean_square + 1e-06) * norm_gain.reshape(head_count, head_dim)
    )
    return rescaled_hidden.reshape(tok_rows, columns).astype(jnp.bfloat16)


def attend(my_queries, query_places, key_rows, value_rows, doc_ids, span_factor):
    all_rows, unit_heads, head_dim = key_rows.shape
    length = my_queries.shape[0]
    tile = min(512, length)
    span = tile * span_factor
    pad_key = jnp.concatenate(
        [
            jnp.zeros((WINDOW, unit_heads, head_dim), jnp.bfloat16),
            key_rows,
            jnp.zeros((span, unit_heads, head_dim), jnp.bfloat16),
        ]
    )
    pad_value = jnp.concatenate(
        [
            jnp.zeros((WINDOW, unit_heads, head_dim), jnp.bfloat16),
            value_rows,
            jnp.zeros((span, unit_heads, head_dim), jnp.bfloat16),
        ]
    )
    pad_docs = jnp.concatenate(
        [jnp.full((WINDOW,), -1, dtype=jnp.int32), doc_ids, jnp.full((span,), -1, dtype=jnp.int32)]
    )

    def one_tile(tile_index):
        tile_rows = lax.dynamic_slice_in_dim(my_queries, tile_index * tile, tile, 0)
        query_pos = lax.dynamic_slice_in_dim(query_places, tile_index * tile, tile, 0)
        first_pos = query_pos[0]
        key_block = lax.dynamic_slice_in_dim(pad_key, first_pos, WINDOW + span, 0)
        value_block = lax.dynamic_slice_in_dim(pad_value, first_pos, WINDOW + span, 0)
        key_docs = lax.dynamic_slice_in_dim(pad_docs, first_pos, WINDOW + span, 0)
        asker_documents = jnp.take(doc_ids, query_pos)
        key_pos = first_pos - WINDOW + jnp.arange(WINDOW + span, dtype=jnp.int32)
        allowed = (
            (key_pos[None, :] <= query_pos[:, None])
            & (key_pos[None, :] > query_pos[:, None] - WINDOW)
            & (key_docs[None, :] == asker_documents[:, None])
        )
        scores = jnp.einsum(
            "qhd,khd->hqk", tile_rows, key_block, preferred_element_type=jnp.float32
        ) * head_dim ** (-0.5)
        scores = jnp.where(allowed[None], scores, -1e30)
        row_peak = jnp.max(scores, axis=-1, keepdims=True)
        exponent = jnp.exp(scores - row_peak)
        weights = (exponent / jnp.sum(exponent, axis=-1, keepdims=True)).astype(jnp.bfloat16)
        return jnp.einsum(
            "hqk,khd->qhd", weights, value_block, preferred_element_type=jnp.float32
        ).astype(jnp.bfloat16)

    tiles_out = lax.map(one_tile, jnp.arange(length // tile, dtype=jnp.int32))
    return tiles_out.reshape(length, unit_heads, head_dim)


def body(gla_query, gla_key, gla_value, log_gates, norm_gain, attn_query, attn_key, doc_blocks):
    tok_rows, columns = attn_query.shape
    head_count = log_gates.shape[1]
    head_dim = columns // head_count
    devices = lax.axis_size("ctx")
    copies = max(1, devices // head_count)
    per_unit = max(1, head_count // devices)
    groups = head_count // per_unit
    share_rows = tok_rows // copies

    def to_heads(rows_in):
        spread_rows = rows_in.reshape(tok_rows, head_count, 1, head_dim)
        spread_rows = jnp.broadcast_to(spread_rows, (tok_rows, head_count, copies, head_dim))
        return spread_rows.reshape(tok_rows, devices, per_unit * head_dim)

    shared = attn_query.reshape(copies, share_rows, groups, per_unit * head_dim).transpose(
        1, 2, 0, 3
    )
    sent_query = shared.reshape(share_rows, devices, per_unit * head_dim)
    gla_mixed = gla_layer(gla_query, gla_key, gla_value, log_gates, norm_gain, doc_blocks)
    moved_query, moved_key, moved_value = (
        lax.all_to_all(sent_query, "ctx", split_axis=1, concat_axis=0, tiled=True),
        lax.all_to_all(to_heads(attn_key), "ctx", split_axis=1, concat_axis=0, tiled=True),
        lax.all_to_all(to_heads(gla_mixed), "ctx", split_axis=1, concat_axis=0, tiled=True),
    )
    all_rows = devices * tok_rows
    unit_shape = (all_rows, per_unit, head_dim)
    moved_query = moved_query.reshape(-1, per_unit, head_dim)
    moved_key = moved_key.reshape(unit_shape)
    moved_value = moved_value.reshape(unit_shape)
    doc_ends = jnp.cumsum(doc_blocks) * BLOCK
    positions = jnp.arange(all_rows, dtype=jnp.int32)
    doc_ids = jnp.sum((positions[:, None] >= doc_ends[None, :]).astype(jnp.int32), axis=1)
    local_replica = lax.axis_index("ctx") % copies
    query_places = (
        jnp.arange(devices, dtype=jnp.int32)[:, None] * tok_rows
        + local_replica * share_rows
        + jnp.arange(share_rows, dtype=jnp.int32)[None, :]
    ).reshape(-1)
    result = attend(moved_query, query_places, moved_key, moved_value, doc_ids, copies)
    outgoing = result.reshape(devices, share_rows, 1, per_unit * head_dim)
    returned = lax.all_to_all(outgoing, "ctx", split_axis=0, concat_axis=2, tiled=True)
    regrouped = returned.reshape(share_rows, groups, copies, per_unit, head_dim).transpose(
        2, 0, 1, 3, 4
    )
    attended = regrouped.reshape(tok_rows, head_count, head_dim)
    return (gla_mixed, attended.reshape(tok_rows, columns))


def scalar_layout(docs, place, pieces):
    end, kind, index, start = jnp.int32(0), jnp.int32(0), jnp.int32(0), jnp.int32(0)
    for d in range(docs.shape[0]):
        length = docs[d]
        inside = (place >= end) & (place < end + length)
        found = jnp.where(length == pieces, 2, jnp.where(length == 2, 1, 0))
        kind = jnp.where(inside, found, kind)
        index = jnp.where(inside, place - end, index)
        start = jnp.where(inside, end, start)
        end = end + length
    return kind, index, start


def place_body(docs, meta):
    pieces = lax.axis_size("ctx") // 2
    kind, index, start = scalar_layout(docs, lax.axis_index("ctx"), pieces)
    alone = lax.axis_size("ctx") - pieces + 3
    meta[0] = jnp.where(kind == 2, start, jnp.where(kind == 1, alone - 2 + start % 2, alone))
    meta[1] = kind
    meta[2] = index
    meta[3] = start


def find_place(docs):
    small = pl.BlockSpec(memory_space=pltpu.SMEM)
    return pl.pallas_call(
        place_body,
        in_specs=[small],
        out_specs=small,
        out_shape=jax.ShapeDtypeStruct((4,), jnp.int32),
        compiler_params=pltpu.CompilerParams(vmem_limit_bytes=ROOM),
        name="place",
    )(pltpu.with_memory_space_constraint(docs, pltpu.HBM))


def pack_body(gq, gk, gv, aq, ak, gates, out, loaded, arrived):
    pieces, tall, dim = out.shape
    rows, columns = gq.shape
    per = columns // dim // pieces
    copies = [
        pltpu.make_async_copy(source, loaded.at[i], arrived.at[i])
        for i, source in enumerate((gq, gk, gv, aq, ak))
    ]
    for copy in copies:
        copy.start()
    below = lax.broadcasted_iota(jnp.int32, (rows, rows), 0)
    until = lax.broadcasted_iota(jnp.int32, (rows, rows), 1)
    sums = jnp.dot(
        gates[...],
        (below <= until).astype(jnp.float32),
        precision=lax.Precision.HIGHEST,
        preferred_element_type=jnp.float32,
    )
    place = lax.broadcasted_iota(jnp.int32, (tall - 5 * rows * per, rows), 0)
    for j in range(pieces):
        tile = jnp.zeros(place.shape, jnp.float32)
        for h in range(per):
            line = sums[j * per + h : j * per + h + 1, :] * LOG2E
            first = line.astype(jnp.bfloat16).astype(jnp.float32)
            rest = line - first
            second = rest.astype(jnp.bfloat16).astype(jnp.float32)
            for i, share in enumerate((first, second, rest - second)):
                tile = jnp.where(place == 3 * h + i, share, tile)
        out[j, 5 * rows * per :] = tile.astype(jnp.bfloat16)

    for i, copy in enumerate(copies):
        copy.wait()

        def piece(j, carry):
            for h in range(per):
                own = pl.ds(pl.multiple_of((j * per + h) * dim, dim), dim)
                out[j, (5 * h + i) * rows : (5 * h + i + 1) * rows] = loaded[i, :, own]
            return carry

        lax.fori_loop(0, pieces, piece, 0)


def pack(gq, gk, gv, aq, ak, gates):
    rows, columns = gq.shape
    heads = gates.shape[0]
    pieces = lax.axis_size("ctx") // 2
    per = heads // pieces
    tall = 5 * rows * per + pl.cdiv(3 * per, 16) * 16
    whole = pl.BlockSpec(memory_space=pltpu.VMEM)
    return pl.pallas_call(
        pack_body,
        in_specs=[pl.BlockSpec(memory_space=pltpu.HBM)] * 5 + [whole],
        out_specs=whole,
        out_shape=jax.ShapeDtypeStruct((pieces, tall, columns // heads), jnp.bfloat16),
        scratch_shapes=[pltpu.VMEM((5, rows, columns), jnp.bfloat16), pltpu.SemaphoreType.DMA((5,))],
        compiler_params=pltpu.CompilerParams(vmem_limit_bytes=ROOM),
        name="pack",
    )(gq, gk, gv, aq, ak, gates)


def mm(a, b):
    return jnp.dot(a, b, preferred_element_type=jnp.float32)


def mm_t(a, b):
    return lax.dot_general(a, b, (((1,), (1,)), ((), ())), preferred_element_type=jnp.float32)


def mix_body(meta, source, gain, out, got, values, arrived):
    pieces, _, dim = got.shape
    rows = values.shape[2]
    copies = [pltpu.make_async_copy(source.at[n], got.at[n], arrived.at[n]) for n in range(pieces)]
    for copy in copies:
        copy.start()
    kind, index = meta[1], meta[2]
    half = pieces // 2
    at, group = [], []
    for n in range(pieces):
        slot = jnp.where(kind == 1, (n % 2) * half + n // 2, n)
        at.append(slot)
        group.append(jnp.where(kind == 2, index, jnp.where(kind == 1, half * index + n // 2, n)))

    heads = range(values.shape[0])
    values[:, :, :, dim:] = jnp.ones(values.shape[:3] + (dim,), jnp.bfloat16)

    def part(at, h, n, i):
        return got[at[n], (5 * h + i) * rows : (5 * h + i + 1) * rows]

    row = lax.broadcasted_iota(jnp.int32, (2 * rows, 2 * rows), 0)
    col = lax.broadcasted_iota(jnp.int32, (2 * rows, 2 * rows), 1)
    wide = row >= col
    causal = wide[:rows, :rows]

    def recur(at, group, h, n, states, keep):
        state = states[h]
        query, key, value = part(at, h, n, 0), part(at, h, n, 1), part(at, h, n, 2)
        shares = got[at[n], 5 * rows * len(heads) :].astype(jnp.float32)
        place = lax.broadcasted_iota(jnp.int32, shares.shape, 0)
        shares = jnp.where((place >= 3 * h) & (place < 3 * h + 3), shares, 0.0)
        line = jnp.sum(shares, axis=0, keepdims=True)
        across = jnp.broadcast_to(line, (rows, rows))
        products = mm_t(query, key)
        yield
        down = across.T
        turned = key.astype(jnp.float32).T
        yield
        last = down[rows - 1 : rows, :]
        tail = (turned * jnp.exp2(last - line)).astype(jnp.bfloat16)
        added = mm(tail, value)
        yield
        weight = jnp.where(causal, jnp.exp2(down - across), 0.0)
        inside = (products * weight).astype(jnp.bfloat16)
        yield
        if state is None:
            mixture = mm(inside, value)
            states[h] = added
        else:
            if keep is not None:
                state = state * keep
            far = (query.astype(jnp.float32) * jnp.exp2(down)).astype(jnp.bfloat16)
            mixture = mm(
                jnp.concatenate([inside, far], axis=1),
                jnp.concatenate([value, state.astype(jnp.bfloat16)], axis=0),
            )
            states[h] = state * jnp.exp2(last) + added
        yield
        square = jnp.mean(mixture * mixture, axis=-1, keepdims=True)
        yield
        mixed = mixture * lax.rsqrt(square + 1e-06 * dim) * gain[h, pl.ds(group[n], 1), :]
        mixed = mixed.astype(jnp.bfloat16)
        values[h, n, :, :dim] = mixed
        out[at[n], h, :rows] = mixed

    def attend_pair(at, h, first, n, open_):
        queries = jnp.concatenate([part(at, h, n - 1, 3), part(at, h, n, 3)], axis=0)
        keys = jnp.concatenate([part(at, h, m, 4) for m in range(first, n + 1)], axis=0)
        scores = mm_t(queries, keys)
        edge = (n - 1 - first) * rows
        near = jnp.where(open_, scores[:, edge:], -1e30)
        yield
        top = jnp.maximum(near[:, :rows], near[:, rows:])
        for m in range(edge // rows):
            top = jnp.maximum(top, scores[:, m * rows : (m + 1) * rows])
        yield
        peak = jnp.max(top, axis=-1, keepdims=True)
        yield
        parts = [near[:, :rows], near[:, rows:]]
        parts = [scores[:, m * rows : (m + 1) * rows] for m in range(edge // rows)] + parts
        exponents = []
        for s in parts:
            exponents.append(jnp.exp2((s - peak) * (dim ** (-0.5) * LOG2E)).astype(jnp.bfloat16))
            if len(exponents) % 2 == 0:
                yield
        stacked = values[h, first : n + 1].reshape((n + 1 - first) * rows, 2 * dim)
        both = mm(jnp.concatenate(exponents, axis=1), stacked)
        yield
        result = (both[:, :dim] / both[:, dim:]).astype(jnp.bfloat16)
        out[at[n - 1], h, rows:] = result[:rows]
        out[at[n], h, rows:] = result[rows:]

    def together(runs):
        while runs:
            runs = [run for run in runs if next(run, True) is None]

    def in_one():
        states = [None for _ in heads]
        straight = list(range(pieces))
        whole = [index] * pieces
        waiting = []
        for n in range(pieces):
            for copy in (copies[:2], copies[2:4], copies[4:])[n // 2] if n in (0, 2, 4) else ():
                copy.wait()
            late = waiting if n % 2 == 0 else []
            together([recur(straight, whole, h, n, states, None) for h in heads] + late)
            if n % 2:
                waiting = [attend_pair(straight, h, 0, n, wide) for h in heads]
        together(waiting)

    def in_twos():
        for copy in copies:
            copy.wait()
        keep = (kind == 1).astype(jnp.float32)
        reach = jnp.where(kind == 1, 2 * rows, rows)
        narrow = wide & ((row < rows) | (col >= 2 * rows - reach))
        for n in range(0, pieces, 2):
            states = [None for _ in heads]
            for m, link in ((n, None), (n + 1, keep)):
                together([recur(at, group, h, m, states, link) for h in heads])
            together([attend_pair(at, h, n, n + 1, narrow) for h in heads])

    lax.cond(kind == 2, in_one, in_twos)


def mix(meta, got, norm_gain, rows):
    pieces, tall, dim = got.shape
    per = norm_gain.shape[0] // dim // pieces
    gain = norm_gain.reshape(pieces, per, dim).transpose(1, 0, 2)
    whole = pl.BlockSpec(memory_space=pltpu.VMEM)
    return pl.pallas_call(
        mix_body,
        in_specs=[
            pl.BlockSpec(memory_space=pltpu.SMEM),
            pl.BlockSpec(memory_space=pl.ANY),
            whole,
        ],
        out_specs=whole,
        out_shape=jax.ShapeDtypeStruct((pieces, per, 2 * rows, dim), jnp.bfloat16),
        scratch_shapes=[
            pltpu.VMEM(got.shape, jnp.bfloat16),
            pltpu.VMEM((per, pieces, rows, 2 * dim), jnp.bfloat16),
            pltpu.SemaphoreType.DMA((pieces,)),
        ],
        compiler_params=pltpu.CompilerParams(vmem_limit_bytes=ROOM),
        name="mix",
    )(meta, got, gain)


def unpack_body(got, first, second, lined, sent):
    pieces, per, tall, dim = got.shape
    width = per * dim
    copies = []
    for j in range(pieces):
        columns = slice(j * width, (j + 1) * width)
        for i, target in enumerate((first, second)):
            for h in range(per):
                lined[i, j, :, h * dim : (h + 1) * dim] = got[j, h, i * tall // 2 : (i + 1) * tall // 2]
            copies.append(pltpu.make_async_copy(lined.at[i, j], target.at[:, columns], sent.at[i, j]))
            copies[-1].start()
    for copy in copies:
        copy.wait()


def unpack(got):
    pieces, per, tall, dim = got.shape
    shape = jax.ShapeDtypeStruct((tall // 2, pieces * per * dim), jnp.bfloat16)
    return pl.pallas_call(
        unpack_body,
        in_specs=[pl.BlockSpec(memory_space=pltpu.VMEM)],
        out_specs=[pl.BlockSpec(memory_space=pltpu.HBM)] * 2,
        out_shape=[shape, shape],
        scratch_shapes=[
            pltpu.VMEM((2, pieces, tall // 2, per * dim), jnp.bfloat16),
            pltpu.SemaphoreType.DMA((2, pieces)),
        ],
        compiler_params=pltpu.CompilerParams(vmem_limit_bytes=ROOM),
        name="unpack",
    )(got)


def document_body(gla_query, gla_key, gla_value, log_gates, norm_gain, attn_query, attn_key, doc_blocks):
    devices = lax.axis_size("ctx")
    pieces = devices // 2
    meta = find_place(doc_blocks)
    held = (gla_query, gla_key, gla_value, attn_query, attn_key, log_gates.T)
    members = []
    for start in range(devices - pieces + 1):
        inside = list(range(start, start + pieces))
        members.append([inside, [i for i in range(devices) if i not in inside]])
    for start in range(2):
        members.append([[(i + start) % devices, (i + start + 1) % devices] for i in range(0, devices, 2)])

    def exchange(x, groups):
        return lax.all_to_all(x, "ctx", split_axis=0, concat_axis=0, tiled=True, axis_index_groups=groups)

    def outward(groups):
        return lambda *held: exchange(pack(*held), groups)

    def homeward(groups):
        return lambda x: exchange(x, groups)

    got = lax.switch(meta[0], [outward(groups) for groups in members] + [pack], *held)
    mixed = mix(meta, got, norm_gain, gla_query.shape[0])
    back = lax.switch(meta[0], [homeward(groups) for groups in members] + [lambda x: x], mixed)
    return tuple(unpack(back))


def solution(mesh):
    placed = (
        P(("grp", "ctx"), None),
        P(("grp", "ctx"), None),
        P(("grp", "ctx"), None),
        P(("grp", "ctx"), None),
        P(),
        P(("grp", "ctx"), None),
        P(("grp", "ctx"), None),
        P("grp"),
    )
    parts, devices = mesh.shape["grp"], mesh.shape["ctx"]

    def step(gla_query, gla_key, gla_value, log_gates, norm_gain, attn_query, attn_key, doc_blocks):
        blocks = gla_query.shape[0] // parts // BLOCK
        documents = doc_blocks.shape[0] // parts
        longest = blocks // 2
        spare = blocks - longest - (documents - 1)
        heads = log_gates.shape[1]
        simple = blocks == devices and spare == 1 and heads % longest == 0 and longest * BLOCK <= WINDOW
        simple = simple and longest > 2 and longest % 2 == 0
        return jax.shard_map(
            document_body if simple else body,
            mesh=mesh,
            in_specs=placed,
            out_specs=(P(("grp", "ctx"), None), P(("grp", "ctx"), None)),
            check_vma=False,
        )(gla_query, gla_key, gla_value, log_gates, norm_gain, attn_query, attn_key, doc_blocks)

    return step
```

```python
import functools

import jax
import jax.numpy as jnp
from jax import lax
from jax.experimental import pallas as pl
from jax.experimental.pallas import tpu as pltpu
from jax.sharding import PartitionSpec as P

BLOCK = 128
WINDOW = 2048
LOG2E = 1.4426950408889634
ROOM = 24 * 2**20


def entering_2(part, axis, combine, identity):
    place = lax.axis_index(axis)
    gathered = jax.tree.map(lambda a: lax.all_gather(a, axis), part)
    state = jax.tree.map(lambda a, e: jnp.zeros_like(a) + jnp.asarray(e, a.dtype), part, identity)

    def one(turn, state):
        return combine(
            state, jax.tree.map(lambda a: lax.dynamic_index_in_dim(a, turn, 0, False), gathered)
        )

    return lax.fori_loop(0, place, one, state)


def compose(earlier, later):
    return (earlier[0] * later[0], later[0][:, None, None] * earlier[1] + later[1])


def gla_layer(gla_query, gla_key, gla_value, log_gates, norm_gain, doc_blocks):
    tok_rows, columns = gla_query.shape
    head_count = log_gates.shape[1]
    head_dim = columns // head_count
    block_count = tok_rows // BLOCK
    offset = lax.axis_index("ctx") * tok_rows
    doc_ends = jnp.cumsum(doc_blocks) * BLOCK
    starts = doc_ends - doc_blocks * BLOCK
    block_offsets = offset + jnp.arange(block_count, dtype=jnp.int32) * BLOCK
    resets = jnp.any(block_offsets[:, None] == starts[None, :], axis=1).astype(jnp.float32)
    shaped = (block_count, BLOCK, head_count, head_dim)
    query_rows = gla_query.reshape(shaped)
    key_rows = gla_key.reshape(shaped)
    float_query = query_rows.astype(jnp.float32) * head_dim ** (-0.5)
    float_key = key_rows.astype(jnp.float32)
    float_value = gla_value.reshape(shaped).astype(jnp.float32)
    gate_sums = jnp.cumsum(log_gates.reshape(block_count, BLOCK, head_count), axis=1)
    block_last = gate_sums[:, -1, :]
    by_head = gate_sums.transpose(0, 2, 1)
    causal = (jnp.arange(BLOCK)[:, None] >= jnp.arange(BLOCK)[None, :])[None, None]
    gaps = by_head[:, :, :, None] - by_head[:, :, None, :]
    weight = jnp.where(causal, jnp.exp(jnp.where(causal, gaps, 0.0)), 0.0)
    raw_scores = jnp.einsum(
        "cthd,cshd->chts", query_rows, key_rows, preferred_element_type=jnp.float32
    )
    scores = raw_scores * head_dim ** (-0.5) * weight
    inner_part = jnp.einsum("chts,cshd->cthd", scores, float_value, precision=lax.Precision.HIGHEST)
    tails = jnp.exp(block_last[:, None, :] - gate_sums)
    local_state = jnp.einsum(
        "cshd,cshe->chde",
        float_key * tails[..., None],
        float_value,
        precision=lax.Precision.HIGHEST,
    )
    decays = jnp.exp(block_last) * (1.0 - resets)[:, None]
    total_decay = jnp.ones((head_count,), jnp.float32)
    total_state = jnp.zeros((head_count, head_dim, head_dim), jnp.float32)
    block_id = 0
    total_decay, total_state = compose(
        (total_decay, total_state), (decays[block_id], local_state[block_id])
    )
    identity = (
        jnp.ones((head_count,), jnp.float32),
        jnp.zeros((head_count, head_dim, head_dim), jnp.float32),
    )
    incoming = entering_2((total_decay, total_state), "ctx", compose, identity)
    carried = incoming[1]
    block_id = 0
    entering = carried * (1.0 - resets[block_id])
    scaled_query = float_query[block_id] * jnp.exp(gate_sums[block_id])[..., None]
    outer_parts = [
        jnp.einsum("thd,hde->the", scaled_query, entering, precision=lax.Precision.HIGHEST)
    ]
    mixture = inner_part + jnp.stack(outer_parts)
    mean_square = jnp.mean(mixture * mixture, axis=-1, keepdims=True)
    rescaled_hidden = (
        mixture * lax.rsqrt(mean_square + 1e-06) * norm_gain.reshape(head_count, head_dim)
    )
    return rescaled_hidden.reshape(tok_rows, columns).astype(jnp.bfloat16)


def attend(my_queries, query_places, key_rows, value_rows, doc_ids, span_factor):
    all_rows, unit_heads, head_dim = key_rows.shape
    length = my_queries.shape[0]
    tile = min(512, length)
    span = tile * span_factor
    pad_key = jnp.concatenate(
        [
            jnp.zeros((WINDOW, unit_heads, head_dim), jnp.bfloat16),
            key_rows,
            jnp.zeros((span, unit_heads, head_dim), jnp.bfloat16),
        ]
    )
    pad_value = jnp.concatenate(
        [
            jnp.zeros((WINDOW, unit_heads, head_dim), jnp.bfloat16),
            value_rows,
            jnp.zeros((span, unit_heads, head_dim), jnp.bfloat16),
        ]
    )
    pad_docs = jnp.concatenate(
        [jnp.full((WINDOW,), -1, dtype=jnp.int32), doc_ids, jnp.full((span,), -1, dtype=jnp.int32)]
    )

    def one_tile(tile_index):
        tile_rows = lax.dynamic_slice_in_dim(my_queries, tile_index * tile, tile, 0)
        query_pos = lax.dynamic_slice_in_dim(query_places, tile_index * tile, tile, 0)
        first_pos = query_pos[0]
        key_block = lax.dynamic_slice_in_dim(pad_key, first_pos, WINDOW + span, 0)
        value_block = lax.dynamic_slice_in_dim(pad_value, first_pos, WINDOW + span, 0)
        key_docs = lax.dynamic_slice_in_dim(pad_docs, first_pos, WINDOW + span, 0)
        asker_documents = jnp.take(doc_ids, query_pos)
        key_pos = first_pos - WINDOW + jnp.arange(WINDOW + span, dtype=jnp.int32)
        allowed = (
            (key_pos[None, :] <= query_pos[:, None])
            & (key_pos[None, :] > query_pos[:, None] - WINDOW)
            & (key_docs[None, :] == asker_documents[:, None])
        )
        scores = jnp.einsum(
            "qhd,khd->hqk", tile_rows, key_block, preferred_element_type=jnp.float32
        ) * head_dim ** (-0.5)
        scores = jnp.where(allowed[None], scores, -1e30)
        row_peak = jnp.max(scores, axis=-1, keepdims=True)
        exponent = jnp.exp(scores - row_peak)
        weights = (exponent / jnp.sum(exponent, axis=-1, keepdims=True)).astype(jnp.bfloat16)
        return jnp.einsum(
            "hqk,khd->qhd", weights, value_block, preferred_element_type=jnp.float32
        ).astype(jnp.bfloat16)

    tiles_out = lax.map(one_tile, jnp.arange(length // tile, dtype=jnp.int32))
    return tiles_out.reshape(length, unit_heads, head_dim)


def body(gla_query, gla_key, gla_value, log_gates, norm_gain, attn_query, attn_key, doc_blocks):
    tok_rows, columns = attn_query.shape
    head_count = log_gates.shape[1]
    head_dim = columns // head_count
    devices = lax.axis_size("ctx")
    copies = max(1, devices // head_count)
    per_unit = max(1, head_count // devices)
    groups = head_count // per_unit
    share_rows = tok_rows // copies

    def to_heads(rows_in):
        spread_rows = rows_in.reshape(tok_rows, head_count, 1, head_dim)
        spread_rows = jnp.broadcast_to(spread_rows, (tok_rows, head_count, copies, head_dim))
        return spread_rows.reshape(tok_rows, devices, per_unit * head_dim)

    shared = attn_query.reshape(copies, share_rows, groups, per_unit * head_dim).transpose(
        1, 2, 0, 3
    )
    sent_query = shared.reshape(share_rows, devices, per_unit * head_dim)
    gla_mixed = gla_layer(gla_query, gla_key, gla_value, log_gates, norm_gain, doc_blocks)
    moved_query, moved_key, moved_value = (
        lax.all_to_all(sent_query, "ctx", split_axis=1, concat_axis=0, tiled=True),
        lax.all_to_all(to_heads(attn_key), "ctx", split_axis=1, concat_axis=0, tiled=True),
        lax.all_to_all(to_heads(gla_mixed), "ctx", split_axis=1, concat_axis=0, tiled=True),
    )
    all_rows = devices * tok_rows
    unit_shape = (all_rows, per_unit, head_dim)
    moved_query = moved_query.reshape(-1, per_unit, head_dim)
    moved_key = moved_key.reshape(unit_shape)
    moved_value = moved_value.reshape(unit_shape)
    doc_ends = jnp.cumsum(doc_blocks) * BLOCK
    positions = jnp.arange(all_rows, dtype=jnp.int32)
    doc_ids = jnp.sum((positions[:, None] >= doc_ends[None, :]).astype(jnp.int32), axis=1)
    local_replica = lax.axis_index("ctx") % copies
    query_places = (
        jnp.arange(devices, dtype=jnp.int32)[:, None] * tok_rows
        + local_replica * share_rows
        + jnp.arange(share_rows, dtype=jnp.int32)[None, :]
    ).reshape(-1)
    result = attend(moved_query, query_places, moved_key, moved_value, doc_ids, copies)
    outgoing = result.reshape(devices, share_rows, 1, per_unit * head_dim)
    returned = lax.all_to_all(outgoing, "ctx", split_axis=0, concat_axis=2, tiled=True)
    regrouped = returned.reshape(share_rows, groups, copies, per_unit, head_dim).transpose(
        2, 0, 1, 3, 4
    )
    attended = regrouped.reshape(tok_rows, head_count, head_dim)
    return (gla_mixed, attended.reshape(tok_rows, columns))


def scalar_layout(docs, place, pieces):
    end, kind, index, start = jnp.int32(0), jnp.int32(0), jnp.int32(0), jnp.int32(0)
    for d in range(docs.shape[0]):
        length = docs[d]
        inside = (place >= end) & (place < end + length)
        found = jnp.where(length == pieces, 2, jnp.where(length == 2, 1, 0))
        kind = jnp.where(inside, found, kind)
        index = jnp.where(inside, place - end, index)
        start = jnp.where(inside, end, start)
        end = end + length
    return kind, index, start


def place_body(docs, meta):
    pieces = lax.axis_size("ctx") // 2
    kind, index, start = scalar_layout(docs, lax.axis_index("ctx"), pieces)
    alone = lax.axis_size("ctx") - pieces + 3
    meta[0] = jnp.where(kind == 2, start, jnp.where(kind == 1, alone - 2 + start % 2, alone))
    meta[1] = kind
    meta[2] = index
    meta[3] = start


def find_place(docs):
    small = pl.BlockSpec(memory_space=pltpu.SMEM)
    return pl.pallas_call(
        place_body,
        in_specs=[small],
        out_specs=small,
        out_shape=jax.ShapeDtypeStruct((4,), jnp.int32),
        compiler_params=pltpu.CompilerParams(vmem_limit_bytes=ROOM),
        name="place",
    )(pltpu.with_memory_space_constraint(docs, pltpu.HBM))


def pack_body(gq, gk, gv, aq, ak, gates, out, loaded, arrived):
    pieces, tall, dim = out.shape
    rows, columns = gq.shape
    per = columns // dim // pieces
    copies = [
        pltpu.make_async_copy(source, loaded.at[i], arrived.at[i])
        for i, source in enumerate((gq, gk, gv, aq, ak))
    ]
    for copy in copies:
        copy.start()
    below = lax.broadcasted_iota(jnp.int32, (rows, rows), 0)
    until = lax.broadcasted_iota(jnp.int32, (rows, rows), 1)
    sums = jnp.dot(
        gates[...],
        (below <= until).astype(jnp.float32),
        precision=lax.Precision.HIGHEST,
        preferred_element_type=jnp.float32,
    )
    place = lax.broadcasted_iota(jnp.int32, (tall - 5 * rows * per, rows), 0)
    for j in range(pieces):
        tile = jnp.zeros(place.shape, jnp.float32)
        for h in range(per):
            line = sums[j * per + h : j * per + h + 1, :] * LOG2E
            first = line.astype(jnp.bfloat16).astype(jnp.float32)
            rest = line - first
            second = rest.astype(jnp.bfloat16).astype(jnp.float32)
            for i, share in enumerate((first, second, rest - second)):
                tile = jnp.where(place == 3 * h + i, share, tile)
        out[j, 5 * rows * per :] = tile.astype(jnp.bfloat16)

    for i, copy in enumerate(copies):
        copy.wait()

        def piece(j, carry):
            for h in range(per):
                own = pl.ds(pl.multiple_of((j * per + h) * dim, dim), dim)
                out[j, (5 * h + i) * rows : (5 * h + i + 1) * rows] = loaded[i, :, own]
            return carry

        lax.fori_loop(0, pieces, piece, 0)


def pack(gq, gk, gv, aq, ak, gates):
    rows, columns = gq.shape
    heads = gates.shape[0]
    pieces = lax.axis_size("ctx") // 2
    per = heads // pieces
    tall = 5 * rows * per + pl.cdiv(3 * per, 16) * 16
    whole = pl.BlockSpec(memory_space=pltpu.VMEM)
    return pl.pallas_call(
        pack_body,
        in_specs=[pl.BlockSpec(memory_space=pltpu.HBM)] * 5 + [whole],
        out_specs=whole,
        out_shape=jax.ShapeDtypeStruct((pieces, tall, columns // heads), jnp.bfloat16),
        scratch_shapes=[pltpu.VMEM((5, rows, columns), jnp.bfloat16), pltpu.SemaphoreType.DMA((5,))],
        compiler_params=pltpu.CompilerParams(vmem_limit_bytes=ROOM),
        name="pack",
    )(gq, gk, gv, aq, ak, gates)


def mm(a, b):
    return jnp.dot(a, b, preferred_element_type=jnp.float32)


def mm_t(a, b):
    return lax.dot_general(a, b, (((1,), (1,)), ((), ())), preferred_element_type=jnp.float32)


def mix_body(meta, source, gain, out, got, values, arrived):
    pieces, _, dim = got.shape
    rows = values.shape[2]
    copies = [pltpu.make_async_copy(source.at[n], got.at[n], arrived.at[n]) for n in range(pieces)]
    for copy in copies:
        copy.start()
    kind, index = meta[1], meta[2]
    half = pieces // 2
    at, group = [], []
    for n in range(pieces):
        slot = jnp.where(kind == 1, (n % 2) * half + n // 2, n)
        at.append(slot)
        group.append(jnp.where(kind == 2, index, jnp.where(kind == 1, half * index + n // 2, n)))

    heads = range(values.shape[0])
    values[:, :, :, dim:] = jnp.ones(values.shape[:3] + (dim,), jnp.bfloat16)

    def part(at, h, n, i):
        return got[at[n], (5 * h + i) * rows : (5 * h + i + 1) * rows]

    row = lax.broadcasted_iota(jnp.int32, (2 * rows, 2 * rows), 0)
    col = lax.broadcasted_iota(jnp.int32, (2 * rows, 2 * rows), 1)
    wide = row >= col
    causal = wide[:rows, :rows]

    def recur(at, group, h, n, states, keep):
        query, key, value = part(at, h, n, 0), part(at, h, n, 1), part(at, h, n, 2)
        shares = got[at[n], 5 * rows * len(heads) :].astype(jnp.float32)
        place = lax.broadcasted_iota(jnp.int32, shares.shape, 0)
        shares = jnp.where((place >= 3 * h) & (place < 3 * h + 3), shares, 0.0)
        line = jnp.sum(shares, axis=0, keepdims=True)
        across = jnp.broadcast_to(line, (rows, rows))
        products = mm_t(query, key)
        yield
        down = across.T
        turned = key.astype(jnp.float32).T
        yield
        last = down[rows - 1 : rows, :]
        tail = (turned * jnp.exp2(last - line)).astype(jnp.bfloat16)
        added = mm(tail, value)
        yield
        weight = jnp.where(causal, jnp.exp2(down - across), 0.0)
        inside = (products * weight).astype(jnp.bfloat16)
        yield
        state = states[h]
        if state is None:
            mixture = mm(inside, value)
            states[h] = added
        else:
            if keep is not None:
                state = state * keep
            far = (query.astype(jnp.float32) * jnp.exp2(down)).astype(jnp.bfloat16)
            mixture = mm(
                jnp.concatenate([inside, far], axis=1),
                jnp.concatenate([value, state.astype(jnp.bfloat16)], axis=0),
            )
            states[h] = state * jnp.exp2(last) + added
        yield
        square = jnp.mean(mixture * mixture, axis=-1, keepdims=True)
        yield
        mixed = mixture * lax.rsqrt(square + 1e-06 * dim) * gain[h, pl.ds(group[n], 1), :]
        mixed = mixed.astype(jnp.bfloat16)
        values[h, n, :, :dim] = mixed
        out[at[n], h, :rows] = mixed

    def attend_pair(at, h, first, n, open_):
        queries = jnp.concatenate([part(at, h, n - 1, 3), part(at, h, n, 3)], axis=0)
        keys = jnp.concatenate([part(at, h, m, 4) for m in range(first, n + 1)], axis=0)
        scores = mm_t(queries, keys)
        edge = (n - 1 - first) * rows
        near = jnp.where(open_, scores[:, edge:], -1e30)
        yield
        top = jnp.maximum(near[:, :rows], near[:, rows:])
        for m in range(edge // rows):
            top = jnp.maximum(top, scores[:, m * rows : (m + 1) * rows])
        yield
        peak = jnp.max(top, axis=-1, keepdims=True)
        yield
        parts = [near[:, :rows], near[:, rows:]]
        parts = [scores[:, m * rows : (m + 1) * rows] for m in range(edge // rows)] + parts
        exponents = []
        for s in parts:
            exponents.append(jnp.exp2((s - peak) * (dim ** (-0.5) * LOG2E)).astype(jnp.bfloat16))
            if len(exponents) % 2 == 0:
                yield
        stacked = values[h, first : n + 1].reshape((n + 1 - first) * rows, 2 * dim)
        both = mm(jnp.concatenate(exponents, axis=1), stacked)
        yield
        result = (both[:, :dim] / both[:, dim:]).astype(jnp.bfloat16)
        out[at[n - 1], h, rows:] = result[:rows]
        out[at[n], h, rows:] = result[rows:]

    def together(runs):
        while runs:
            runs = [run for run in runs if next(run, True) is None]

    def in_one():
        states = [None for _ in heads]
        straight = list(range(pieces))
        whole = [index] * pieces
        waiting = []
        for n in range(0, pieces, 2):
            for copy in (copies[:2], copies[2:4], copies[4:])[n // 2] if n < 6 else ():
                copy.wait()
            steps = [recur(straight, whole, h, m, states, None) for m in (n, n + 1) for h in heads]
            together(steps + waiting)
            waiting = [attend_pair(straight, h, 0, n + 1, wide) for h in heads]
        together(waiting)

    def in_twos():
        for copy in copies:
            copy.wait()
        keep = (kind == 1).astype(jnp.float32)
        reach = jnp.where(kind == 1, 2 * rows, rows)
        narrow = wide & ((row < rows) | (col >= 2 * rows - reach))
        for n in range(0, pieces, 2):
            states = [None for _ in heads]
            for m, link in ((n, None), (n + 1, keep)):
                together([recur(at, group, h, m, states, link) for h in heads])
            together([attend_pair(at, h, n, n + 1, narrow) for h in heads])

    lax.cond(kind == 2, in_one, in_twos)


def mix(meta, got, norm_gain, rows):
    pieces, tall, dim = got.shape
    per = norm_gain.shape[0] // dim // pieces
    gain = norm_gain.reshape(pieces, per, dim).transpose(1, 0, 2)
    whole = pl.BlockSpec(memory_space=pltpu.VMEM)
    return pl.pallas_call(
        mix_body,
        in_specs=[
            pl.BlockSpec(memory_space=pltpu.SMEM),
            pl.BlockSpec(memory_space=pl.ANY),
            whole,
        ],
        out_specs=whole,
        out_shape=jax.ShapeDtypeStruct((pieces, per, 2 * rows, dim), jnp.bfloat16),
        scratch_shapes=[
            pltpu.VMEM(got.shape, jnp.bfloat16),
            pltpu.VMEM((per, pieces, rows, 2 * dim), jnp.bfloat16),
            pltpu.SemaphoreType.DMA((pieces,)),
        ],
        compiler_params=pltpu.CompilerParams(vmem_limit_bytes=ROOM),
        name="mix",
    )(meta, got, gain)


def unpack_body(got, first, second, lined, sent):
    pieces, per, tall, dim = got.shape
    width = per * dim
    copies = []
    for j in range(pieces):
        columns = slice(j * width, (j + 1) * width)
        for i, target in enumerate((first, second)):
            for h in range(per):
                lined[i, j, :, h * dim : (h + 1) * dim] = got[j, h, i * tall // 2 : (i + 1) * tall // 2]
            copies.append(pltpu.make_async_copy(lined.at[i, j], target.at[:, columns], sent.at[i, j]))
            copies[-1].start()
    for copy in copies:
        copy.wait()


def unpack(got):
    pieces, per, tall, dim = got.shape
    shape = jax.ShapeDtypeStruct((tall // 2, pieces * per * dim), jnp.bfloat16)
    return pl.pallas_call(
        unpack_body,
        in_specs=[pl.BlockSpec(memory_space=pltpu.VMEM)],
        out_specs=[pl.BlockSpec(memory_space=pltpu.HBM)] * 2,
        out_shape=[shape, shape],
        scratch_shapes=[
            pltpu.VMEM((2, pieces, tall // 2, per * dim), jnp.bfloat16),
            pltpu.SemaphoreType.DMA((2, pieces)),
        ],
        compiler_params=pltpu.CompilerParams(vmem_limit_bytes=ROOM),
        name="unpack",
    )(got)


def document_body(gla_query, gla_key, gla_value, log_gates, norm_gain, attn_query, attn_key, doc_blocks):
    devices = lax.axis_size("ctx")
    pieces = devices // 2
    meta = find_place(doc_blocks)
    held = (gla_query, gla_key, gla_value, attn_query, attn_key, log_gates.T)
    members = []
    for start in range(devices - pieces + 1):
        inside = list(range(start, start + pieces))
        members.append([inside, [i for i in range(devices) if i not in inside]])
    for start in range(2):
        members.append([[(i + start) % devices, (i + start + 1) % devices] for i in range(0, devices, 2)])

    def exchange(x, groups):
        return lax.all_to_all(x, "ctx", split_axis=0, concat_axis=0, tiled=True, axis_index_groups=groups)

    def outward(groups):
        return lambda *held: exchange(pack(*held), groups)

    def homeward(groups):
        return lambda x: exchange(x, groups)

    got = lax.switch(meta[0], [outward(groups) for groups in members] + [pack], *held)
    mixed = mix(meta, got, norm_gain, gla_query.shape[0])
    back = lax.switch(meta[0], [homeward(groups) for groups in members] + [lambda x: x], mixed)
    return tuple(unpack(back))


def solution(mesh):
    placed = (
        P(("grp", "ctx"), None),
        P(("grp", "ctx"), None),
        P(("grp", "ctx"), None),
        P(("grp", "ctx"), None),
        P(),
        P(("grp", "ctx"), None),
        P(("grp", "ctx"), None),
        P("grp"),
    )
    parts, devices = mesh.shape["grp"], mesh.shape["ctx"]

    def step(gla_query, gla_key, gla_value, log_gates, norm_gain, attn_query, attn_key, doc_blocks):
        blocks = gla_query.shape[0] // parts // BLOCK
        documents = doc_blocks.shape[0] // parts
        longest = blocks // 2
        spare = blocks - longest - (documents - 1)
        heads = log_gates.shape[1]
        simple = blocks == devices and spare == 1 and heads % longest == 0 and longest * BLOCK <= WINDOW
        simple = simple and longest > 2 and longest % 2 == 0
        return jax.shard_map(
            document_body if simple else body,
            mesh=mesh,
            in_specs=placed,
            out_specs=(P(("grp", "ctx"), None), P(("grp", "ctx"), None)),
            check_vma=False,
        )(gla_query, gla_key, gla_value, log_gates, norm_gain, attn_query, attn_key, doc_blocks)

    return step
```
